256 devices in a mesh: rows: 16 (over x, z_hi, core), params: 16 (over z_lo, y).
Axes of the slice: x: 4, y: 4, z: 8 (z_hi: 2, z_lo: 4; z = z_hi * 4 + z_lo), core: 2. Of those that a mesh axis runs over, the one named last changes fastest.
Arguments:
- jacobian: bfloat16 [32768, 12288], P('rows', 'params'), may hold values from -0.0546875 to 0.0546875
- pattern: int32 [256, 96], P('rows', 'params'), may hold values from 0 to 1, as said below
- row_class: int32 [32768], P('rows'), may hold values from 0 to 15
- class_weight: float32 [16], replicated, may hold values from 0.1 to 10
- probes: bfloat16 [32, 12288], P(None, 'params'), may hold values from -6 to 6
Outputs:
- basis: bfloat16 [32, 12288], P(None, 'params')
The draws below stay inside these ranges and needn't reach their ends.
Inputs may be any that keep to these rules, and one draw needn't show every extreme that they name: `pattern`: 1 marks a nonzero block of the Jacobian, 0 a zero block.
All inputs are finite; a program needn't handle non-finite values.
Results may differ from the reference program's by a relative error of at most 0.0075.
Values may be sent and summed in bfloat16 or wider, within the bound.
A program may use at most 64 MiB of HBM per device.

```python
import math
import jax
import jax.numpy as jnp
from jax import lax

P_SIZE = 12288
BLOCK = 128
PROBES = 32
NCLASS = 16
ITERS = 4
ROWS = 32768
RB = 256
PB = 96


def draw_pattern(key, part):
    base = jax.random.fold_in(key, 23)
    level = jax.random.randint(jax.random.fold_in(base, 1), (1, PB), 15, 96)
    roll = jax.random.randint(jax.random.fold_in(base, 2), (RB, PB), 0, 100)
    return (roll < level).astype(jnp.int32)


def touch_ends(array, own_key, least, high):
    index_at = [jax.random.randint(jax.random.fold_in(own_key, axis), (), 0, length) for axis, length in enumerate(array.shape)]
    widest = array.shape.index(max(array.shape))
    next_to = index_at[:widest] + [(index_at[widest] + 1) % array.shape[widest]] + index_at[widest + 1:]
    return array.at[tuple(index_at)].set(least).at[tuple(next_to)].set(high)


def level_of(stream_key, shape, cuts, low, high):
    level = 1.0
    for position, shards_of in cuts:
        draws = jax.random.uniform(jax.random.fold_in(jax.random.fold_in(stream_key, 6), position), (shards_of,), jnp.float32, low / len(cuts), high / len(cuts))
        level = level * jnp.repeat(jnp.exp(draws), shape[position] // shards_of).reshape((-1,) + (1,) * (len(shape) - 1 - position))
    return level


def scatter_about(rng, shape, scale, limit, cuts=(), held_as=jnp.bfloat16):
    gain = level_of(rng, shape, cuts, -0.22, 0.18) if cuts else 1.0
    entries = jax.random.normal(rng, shape, jnp.float32) * scale * gain
    return jnp.minimum(jnp.maximum(entries, -limit), limit).astype(held_as)


def setup_inputs(seed: int = 0) -> dict:
    keys = jax.random.split(jax.random.key(seed), 6)
    jacobian = scatter_about(keys[0], (ROWS, P_SIZE), P_SIZE ** -0.5, 0.0546875, ((0, 16), (1, 16)))
    pattern = draw_pattern(jax.random.fold_in(keys[5], 71), 0)
    row_class = touch_ends(jax.random.randint(keys[2], (ROWS,), 0, NCLASS), jax.random.fold_in(keys[2], 1), 0, NCLASS - 1).astype(jnp.int32)
    class_weight = jnp.clip(jnp.exp(jax.random.uniform(keys[3], (NCLASS,), jnp.float32, math.log(0.1), math.log(10.0))), 0.1, 10.0)
    probes = scatter_about(keys[4], (PROBES, P_SIZE), 1.0, 6.0, ((1, 16),))
    return dict(jacobian=jacobian, pattern=pattern, row_class=row_class, class_weight=class_weight, probes=probes)


def reference(jacobian, pattern, row_class, class_weight, probes):
    weight = class_weight[row_class]
    block_rows = math.gcd(ROWS, 4096)
    count = ROWS // block_rows

    def one_step(basis_now, unused):

        def add_block(total, index):
            start = (index * block_rows).astype(jnp.int32)
            rows_part = lax.dynamic_slice_in_dim(jacobian, start, block_rows, 0)
            mask_part = lax.dynamic_slice_in_dim(pattern, (start // BLOCK).astype(jnp.int32), block_rows // BLOCK, 0)
            mask_full = jnp.repeat(jnp.repeat(mask_part, BLOCK, axis=0), BLOCK, axis=1)
            masked = rows_part * mask_full.astype(jacobian.dtype)
            zpart = lax.dot_general(basis_now.astype(jnp.float32), masked.astype(jnp.float32), (((1,), (1,)), ((), ())), preferred_element_type=jnp.float32)
            wpart = lax.dynamic_slice_in_dim(weight, start, block_rows, 0)
            vpart = (zpart * wpart[None, :]).astype(jnp.bfloat16)
            return (total + jnp.dot(vpart.astype(jnp.float32), masked.astype(jnp.float32), preferred_element_type=jnp.float32), None)
        ysum, _ = lax.scan(add_block, jnp.zeros((PROBES, P_SIZE), jnp.float32), jnp.arange(count, dtype=jnp.int32))
        gram = jnp.dot(ysum, ysum.T, precision=lax.Precision.HIGHEST)
        lower = jnp.linalg.cholesky(gram)
        solved = lax.linalg.triangular_solve(lower, ysum, left_side=True, lower=True)
        return ((solved * math.sqrt(P_SIZE)).astype(jnp.bfloat16), None)
    basis, _ = lax.scan(one_step, probes, None, length=ITERS)
    return basis
```

```python
import functools
import math

import jax
import jax.numpy as jnp
from jax import lax
from jax.experimental import pallas as pl
from jax.experimental.pallas import tpu as pltpu
from jax.sharding import PartitionSpec as P

P_SIZE = 12288
BLOCK = 128
ITERS = 4
NY, NZ, NX = 4, 4, 4
MESH = pl.DeviceIdType.MESH
BF16, F32 = jnp.bfloat16, jnp.float32


def dot_t(a, b):
    return lax.dot_general(a, b, (((1,), (1,)), ((), ())), preferred_element_type=F32)


def dot(a, b):
    return jnp.dot(a, b, preferred_element_type=F32)


def pack_gram(g):
    return g[0:8] + pltpu.roll(g[8:16], 32, 1) + pltpu.roll(g[16:24], 64, 1) + pltpu.roll(g[24:32], 96, 1)


def scaled_inverse(gp, scale):
    a = jnp.concatenate([gp, pltpu.roll(gp, 96, 1), pltpu.roll(gp, 64, 1), pltpu.roll(gp, 32, 1)], axis=0)
    n = a.shape[0]
    row = lax.broadcasted_iota(jnp.int32, a.shape, 0)
    lane = lax.broadcasted_iota(jnp.int32, a.shape, 1)
    b = jnp.where(lane < n, a, jnp.where(lane - n == row, 1.0, 0.0))
    for j in range(n - 1):
        factor = b[:, j : j + 1] * (1.0 / b[j : j + 1, j : j + 1])
        b = jnp.where(row > j, b - factor * b[j : j + 1, :], b)
    diag = jnp.sum(jnp.where(lane == row, b, 0.0), axis=1, keepdims=True)
    inv = pltpu.roll(b, 128 - n, 1) * (lax.rsqrt(diag) * scale)
    return inv[:, :n]


def kernel(pattern, class_weight, jac, row_class, probes, out, m, w, w16, qpad, yacc,
           za_s, za_r, zb, zc, ga, gb, ya_s, ya_r, yb, yc, yd, load_sem,
           za_ss, za_rs, zb_ss, zb_rs, zc_ss, zc_rs, ga_ss, ga_rs, gb_ss, gb_rs,
           ya_ss, ya_rs, yb_ss, yb_rs, yc_ss, yc_rs, yd_ss, yd_rs):
    rows, params = lax.axis_index("rows"), lax.axis_index("params")
    y, zl = lax.rem(params, NY), lax.div(params, NY)
    core, zh, x = lax.rem(rows, 2), lax.rem(lax.div(rows, 2), 2), lax.div(rows, 4)
    chunk = m.shape[0] // NY
    scale = math.sqrt(P_SIZE)
    pending = []

    y_peer = [{"params": zl * NY + lax.rem(y + d, NY)} for d in range(NY)]
    z_peer = [{"params": lax.rem(zl + d, NZ) * NY + y} for d in range(NZ)]
    x_peer = [{"rows": lax.rem(x + d, NX) * 4 + zh * 2 + core} for d in range(NX)]
    zh_peer = {"rows": x * 4 + (1 - zh) * 2 + core}
    core_peer = {"rows": x * 4 + zh * 2 + (1 - core)}

    def send(src, dst, ssem, rsem, peer):
        copy = pltpu.make_async_remote_copy(
            src_ref=src, dst_ref=dst, send_sem=ssem, recv_sem=rsem, device_id=peer, device_id_type=MESH)
        copy.start()
        pending.append(copy)
        return copy

    loads = []
    for c in range(NY):
        copy = pltpu.make_async_copy(
            jac.at[pl.ds(c * chunk, chunk), :], m.at[pl.ds(c * chunk, chunk), :], load_sem.at[c])
        copy.start()
        loads.append(copy)

    barrier = pltpu.get_barrier_semaphore()
    friends = y_peer[1:] + z_peer[1:] + x_peer[1:] + [zh_peer, core_peer]
    for peer in friends:
        pl.semaphore_signal(barrier, inc=1, device_id=peer, device_id_type=MESH)

    classes = row_class[...]
    weight = jnp.zeros(classes.shape, F32)
    for c in range(class_weight.shape[0]):
        weight = jnp.where(classes == c, class_weight[c], weight)
    w16[...] = weight
    per = chunk // BLOCK
    for c in range(NY):
        for i in range(per):
            w[c, :, i * BLOCK : (i + 1) * BLOCK] = w16[c * per + i : c * per + i + 1, :]
    qpad[...] = jnp.zeros_like(qpad)

    for c in range(NY):
        loads[c].wait()
        for i in range(per):
            r = c * per + i
            for j in range(pattern.shape[1]):
                keep = jnp.full((BLOCK, BLOCK), pattern[r, j].astype(F32)).astype(BF16)
                at = (pl.ds(r * BLOCK, BLOCK), pl.ds(j * BLOCK, BLOCK))
                m[at] = m[at] * keep

    pl.semaphore_wait(barrier, len(friends))

    def rows_of(c):
        return m[pl.ds(pl.multiple_of(c * chunk, chunk), chunk), :]

    def send_gram(k, q):
        qpad[0:32, :] = q
        ga[k, y] = pack_gram(dot_t(q, qpad[...]))
        return [send(ga.at[k, y], ga.at[k, y], ga_ss.at[k, d - 1], ga_rs.at[k, d - 1], y_peer[d])
                for d in (2, 1, 3)]

    def forward_gram(k, copies):
        for copy in copies:
            copy.wait_recv()
        gb[k, zl] = ((ga[k, 0] + ga[k, 1]) + ga[k, 2]) + ga[k, 3]
        return [send(gb.at[k, zl], gb.at[k, zl], gb_ss.at[k, d - 1], gb_rs.at[k, d - 1], z_peer[d])
                for d in (1, 2, 3)]

    def finish_gram(k, copies):
        for copy in copies:
            copy.wait_recv()
        inv = scaled_inverse(((gb[k, 0] + gb[k, 1]) + gb[k, 2]) + gb[k, 3], scale)
        high = inv.astype(BF16)
        low = (inv - high.astype(F32)).astype(BF16)
        return jnp.concatenate([high, low], axis=0)

    def apply(inv2, v):
        u = dot(inv2, v)
        return u[:32] + u[32:]

    q = probes[...]
    for k in range(ITERS):
        a_copies = {}
        for d in (2, 1, 3):
            za_s[k, d - 1] = dot_t(q, rows_of(lax.rem(y + d, NY))).astype(BF16)
            a_copies[d] = send(za_s.at[k, d - 1], za_r.at[k, d - 1], za_ss.at[k, d - 1], za_rs.at[k, d - 1], y_peer[d])
        if k > 0:
            g_copies = send_gram(k - 1, q)
        own = dot_t(q, rows_of(y))
        for d in (1, 3, 2):
            a_copies[d].wait_recv()
            own = own + za_r[k, d - 1].astype(F32)
        zb[k, zl] = own.astype(BF16)
        b_copies = [send(zb.at[k, zl], zb.at[k, zl], zb_ss.at[k, d - 1], zb_rs.at[k, d - 1], z_peer[d])
                    for d in (1, 2, 3)]
        if k > 0:
            g_copies = forward_gram(k - 1, g_copies)
        for copy in b_copies:
            copy.wait_recv()
        total = ((zb[k, 0].astype(F32) + zb[k, 1].astype(F32)) + zb[k, 2].astype(F32)) + zb[k, 3].astype(F32)
        zc[k, y] = total.astype(BF16)
        c_copies = {d: send(zc.at[k, y], zc.at[k, y], zc_ss.at[k, d - 1], zc_rs.at[k, d - 1], y_peer[d])
                    for d in (2, 1, 3)}
        if k > 0:
            inv2 = finish_gram(k - 1, g_copies)
        acc = None
        for d in (0, 1, 3, 2):
            c = lax.rem(y + NY - d, NY)
            if d:
                c_copies[d].wait_recv()
            z = zc[k, c]
            z = z.astype(F32) if k == 0 else apply(inv2, z)
            v = (z * w[c]).astype(BF16)
            part = dot(v, rows_of(c))
            acc = part if acc is None else acc + part
        yacc[0] = acc[:16]
        yacc[1] = acc[16:]
        ya_s[k] = yacc[1 - core].astype(BF16)
        copy = send(ya_s.at[k], ya_r.at[k], ya_ss.at[k], ya_rs.at[k], core_peer)
        copy.wait_recv()
        yb[k, 0] = (yacc[core] + ya_r[k].astype(F32)).astype(BF16)
        copy = send(yb.at[k, 0], yb.at[k, 1], yb_ss.at[k], yb_rs.at[k], zh_peer)
        copy.wait_recv()
        yc[k, x] = (yb[k, 0].astype(F32) + yb[k, 1].astype(F32)).astype(BF16)
        copies = [send(yc.at[k, x], yc.at[k, x], yc_ss.at[k, d - 1], yc_rs.at[k, d - 1], x_peer[d])
                  for d in (2, 1, 3)]
        for copy in copies:
            copy.wait_recv()
        total = ((yc[k, 0].astype(F32) + yc[k, 1].astype(F32)) + yc[k, 2].astype(F32)) + yc[k, 3].astype(F32)
        yd[k, core] = total.astype(BF16)
        copy = send(yd.at[k, core], yd.at[k, core], yd_ss.at[k], yd_rs.at[k], core_peer)
        copy.wait_recv()
        q = jnp.concatenate([yd[k, 0], yd[k, 1]], axis=0)

    g_copies = forward_gram(ITERS - 1, send_gram(ITERS - 1, q))
    inv2 = finish_gram(ITERS - 1, g_copies)
    out[...] = apply(inv2, q).astype(BF16)
    for copy in pending:
        copy.wait_send()


def local(jacobian, pattern, row_class, class_weight, probes):
    nrows, ncols = jacobian.shape
    chunk = nrows // NY
    k = ITERS
    vmem, dma = pltpu.VMEM, pltpu.SemaphoreType.DMA
    return pl.pallas_call(
        kernel,
        out_shape=jax.ShapeDtypeStruct(probes.shape, BF16),
        in_specs=[
            pl.BlockSpec(memory_space=pltpu.SMEM),
            pl.BlockSpec(memory_space=pltpu.SMEM),
            pl.BlockSpec(memory_space=pl.ANY),
            pl.BlockSpec(memory_space=pltpu.VMEM),
            pl.BlockSpec(memory_space=pltpu.VMEM),
        ],
        out_specs=pl.BlockSpec(memory_space=pltpu.VMEM),
        scratch_shapes=[
            vmem((nrows, ncols), BF16), vmem((NY, 1, chunk), F32), vmem((nrows // 128, 128), F32),
            vmem((128, ncols), BF16), vmem((2, 16, ncols), F32),
            vmem((k, 3, 32, chunk), BF16), vmem((k, 3, 32, chunk), BF16),
            vmem((k, NZ, 32, chunk), BF16), vmem((k, NY, 32, chunk), BF16),
            vmem((k, NY, 8, 128), F32), vmem((k, NZ, 8, 128), F32),
            vmem((k, 16, ncols), BF16), vmem((k, 16, ncols), BF16),
            vmem((k, 2, 16, ncols), BF16), vmem((k, NX, 16, ncols), BF16), vmem((k, 2, 16, ncols), BF16),
            dma((NY,)),
            dma((k, 3)), dma((k, 3)), dma((k, 3)), dma((k, 3)), dma((k, 3)), dma((k, 3)),
            dma((k, 3)), dma((k, 3)), dma((k, 3)), dma((k, 3)),
            dma((k,)), dma((k,)), dma((k,)), dma((k,)), dma((k, 3)), dma((k, 3)), dma((k,)), dma((k,)),
        ],
        compiler_params=pltpu.CompilerParams(collective_id=0, has_side_effects=True),
    )(pattern, class_weight, jacobian, row_class.reshape(-1, 128), probes)


def solution(mesh):
    placed = (P("rows", "params"), P("rows", "params"), P("rows"), P(), P(None, "params"))
    return jax.shard_map(
        local, mesh=mesh, in_specs=placed, out_specs=P(None, "params"), check_vma=False
    )
```

```python
import functools
import math

import jax
import jax.numpy as jnp
from jax import lax
from jax.experimental import pallas as pl
from jax.experimental.pallas import tpu as pltpu
from jax.sharding import PartitionSpec as P

P_SIZE = 12288
BLOCK = 128
ITERS = 4
NY, NZ, NX = 4, 4, 4
MESH = pl.DeviceIdType.MESH
BF16, F32 = jnp.bfloat16, jnp.float32


def dot_t(a, b):
    return lax.dot_general(a, b, (((1,), (1,)), ((), ())), preferred_element_type=F32)


def dot(a, b):
    return jnp.dot(a, b, preferred_element_type=F32)


def pack_gram(g):
    return g[0:8] + pltpu.roll(g[8:16], 32, 1) + pltpu.roll(g[16:24], 64, 1) + pltpu.roll(g[24:32], 96, 1)


def scaled_inverse(gp, scale):
    a = jnp.concatenate([gp, pltpu.roll(gp, 96, 1), pltpu.roll(gp, 64, 1), pltpu.roll(gp, 32, 1)], axis=0)
    n = a.shape[0]
    row = lax.broadcasted_iota(jnp.int32, a.shape, 0)
    lane = lax.broadcasted_iota(jnp.int32, a.shape, 1)
    b = jnp.where(lane < n, a, jnp.where(lane - n == row, 1.0, 0.0))
    for j in range(n - 1):
        factor = b[:, j : j + 1] * (1.0 / b[j : j + 1, j : j + 1])
        b = jnp.where(row > j, b - factor * b[j : j + 1, :], b)
    diag = jnp.sum(jnp.where(lane == row, b, 0.0), axis=1, keepdims=True)
    inv = pltpu.roll(b, 128 - n, 1) * (lax.rsqrt(diag) * scale)
    return inv[:, :n]


def kernel(pattern, class_weight, jac, row_class, probes, out, m, w, w16, qpad, yacc, zown,
           za_s, za_r, zc, ga, gb, gc, ys, y1, y2, load_sem,
           za_ss, za_rs, zc_ss, zc_rs, ga_ss, ga_rs, gb_ss, gb_rs, gc_ss, gc_rs,
           y1_ss, y1_rs, y2_ss, y2_rs):
    rows, params = lax.axis_index("rows"), lax.axis_index("params")
    y, zl = lax.rem(params, NY), lax.div(params, NY)
    core, zh, x = lax.rem(rows, 2), lax.rem(lax.div(rows, 2), 2), lax.div(rows, 4)
    group = m.shape[0] // NZ
    per = group // BLOCK
    scale = math.sqrt(P_SIZE)
    pending = []

    def yz_peer(dz, dy):
        return {"params": lax.rem(zl + dz, NZ) * NY + lax.rem(y + dy, NY)}

    def rows_peer(dx, dz, dc):
        return {"rows": lax.rem(x + dx, NX) * 4 + lax.rem(zh + dz, 2) * 2 + lax.rem(core + dc, 2)}

    yz_far = [(2, 2), (2, 1), (2, 3), (2, 0), (3, 2), (3, 1), (3, 3), (3, 0), (1, 2), (1, 1), (1, 3), (1, 0), (0, 2), (0, 1), (0, 3)]
    y1_far = [(0, 1, 1), (0, 1, 0), (0, 0, 1)]
    y2_far = [(2, 0, 1), (2, 0, 0), (1, 0, 1), (3, 0, 1), (1, 0, 0), (3, 0, 0), (0, 0, 1)]

    def send(src, dst, ssem, rsem, peer):
        copy = pltpu.make_async_remote_copy(
            src_ref=src, dst_ref=dst, send_sem=ssem, recv_sem=rsem, device_id=peer, device_id_type=MESH)
        copy.start()
        pending.append(copy)
        return copy

    loads = []
    for c in range(NZ):
        copy = pltpu.make_async_copy(
            jac.at[pl.ds(c * group, group), :], m.at[pl.ds(c * group, group), :], load_sem.at[c])
        copy.start()
        loads.append(copy)

    barrier = pltpu.get_barrier_semaphore()
    friends = [yz_peer(*d) for d in yz_far] + [rows_peer(*d) for d in y1_far + y2_far[:-1]]
    for peer in friends:
        pl.semaphore_signal(barrier, inc=1, device_id=peer, device_id_type=MESH)

    classes = row_class[...]
    weight = jnp.zeros(classes.shape, F32)
    for c in range(class_weight.shape[0]):
        weight = jnp.where(classes == c, class_weight[c], weight)
    w16[...] = weight
    for c in range(NZ):
        for i in range(per):
            w[c, :, i * BLOCK : (i + 1) * BLOCK] = w16[c * per + i : c * per + i + 1, :]
    qpad[...] = jnp.zeros_like(qpad)

    for c in range(NZ):
        loads[c].wait()
        for i in range(per):
            r = c * per + i
            for j in range(pattern.shape[1]):
                keep = jnp.full((BLOCK, BLOCK), pattern[r, j].astype(F32)).astype(BF16)
                at = (pl.ds(r * BLOCK, BLOCK), pl.ds(j * BLOCK, BLOCK))
                m[at] = m[at] * keep

    def rows_of(c):
        return m[pl.ds(pl.multiple_of(c * group, group), group), :]

    def raw_z(k, q, dz):
        part = dot_t(q, rows_of(lax.rem(zl + dz, NZ)))
        for i in range(NY):
            if dz:
                za_s[k, dz, i] = part[:, i * BLOCK : (i + 1) * BLOCK].astype(BF16)
            else:
                za_s[k, 0, i] = part[:, i * BLOCK : (i + 1) * BLOCK].astype(BF16)
                zown[i] = part[:, i * BLOCK : (i + 1) * BLOCK]

    def scatter_z(k, dz):
        copies = []
        for dy in (2, 1, 3, 0):
            if dz or dy:
                i = dz * NY + dy - 1
                copies.append(send(za_s.at[k, dz, lax.rem(y + dy, NY)], za_r.at[k, i],
                                   za_ss.at[k, i], za_rs.at[k, i], yz_peer(dz, dy)))
        return copies

    def gram(q):
        qpad[0:32, :] = q
        return pack_gram(dot_t(q, qpad[...]))

    def scatter_gram(k, q):
        ga[k, y] = gram(q)
        return [send(ga.at[k, y], ga.at[k, y], ga_ss.at[k, d - 1], ga_rs.at[k, d - 1], yz_peer(0, d))
                for d in (2, 1, 3)]

    def forward_gram(k, copies):
        for copy in copies:
            copy.wait_recv()
        gb[k, zl] = ((ga[k, 0] + ga[k, 1]) + ga[k, 2]) + ga[k, 3]
        return [send(gb.at[k, zl], gb.at[k, zl], gb_ss.at[k, d - 1], gb_rs.at[k, d - 1], yz_peer(d, 0))
                for d in (2, 3, 1)]

    def split_inverse(g):
        inv = scaled_inverse(g, scale)
        high = inv.astype(BF16)
        low = (inv - high.astype(F32)).astype(BF16)
        return jnp.concatenate([high, low], axis=0)

    def apply(inv2, v):
        u = dot(inv2, v)
        return u[:32] + u[32:]

    q = probes[...]
    for k in range(ITERS):
        a_copies = []
        if k == 0:
            for dz in (2, 3, 1, 0):
                raw_z(k, q, dz)
            pl.semaphore_wait(barrier, len(friends))
            for dz in (2, 3, 1, 0):
                a_copies += scatter_z(k, dz)
        else:
            for i, dz in enumerate((2, 3, 1, 0)):
                raw_z(k, q, dz)
                a_copies += scatter_z(k, dz)
                if i == 0:
                    g_copies = scatter_gram(k - 1, q)
            g_copies = forward_gram(k - 1, g_copies)
        total = zown[y]
        for copy in a_copies:
            copy.wait_recv()
        for i in range(NY * NZ - 1):
            total = total + za_r[k, i].astype(F32)
        zc[k, params] = total.astype(BF16)
        c_copies = {}
        for dz, dy in yz_far:
            i = dz * NY + dy - 1
            c_copies[dz, dy] = send(zc.at[k, params], zc.at[k, params], zc_ss.at[k, i], zc_rs.at[k, i], yz_peer(dz, dy))
        if k > 0:
            for copy in g_copies:
                copy.wait_recv()
            inv2 = split_inverse(((gb[k - 1, 0] + gb[k - 1, 1]) + gb[k - 1, 2]) + gb[k - 1, 3])
        acc = None
        for dz in (0, 1, 3, 2):
            c = lax.rem(zl + NZ - dz, NZ)
            for dy in range(NY):
                if dz or dy:
                    c_copies[dz, dy].wait_recv()
            z = jnp.concatenate([zc[k, c * NY + i] for i in range(NY)], axis=1)
            z = z.astype(F32) if k == 0 else apply(inv2, z)
            v = (z * w[c]).astype(BF16)
            part = dot(v, rows_of(c))
            acc = part if acc is None else acc + part
        yacc[0] = acc[:16]
        yacc[1] = acc[16:]
        mine = zh * 2 + core
        ys[k] = yacc[1 - core].astype(BF16)
        y1[k, mine] = yacc[core].astype(BF16)
        copies = []
        for i, (dx, dz, dc) in enumerate(y1_far):
            src = ys.at[k] if dc else y1.at[k, mine]
            copies.append(send(src, y1.at[k, mine], y1_ss.at[k, i], y1_rs.at[k, i], rows_peer(dx, dz, dc)))
        for copy in copies:
            copy.wait_recv()
        total = ((y1[k, 0].astype(F32) + y1[k, 1].astype(F32)) + y1[k, 2].astype(F32)) + y1[k, 3].astype(F32)
        y2[k, x, core] = total.astype(BF16)
        copies = [send(y2.at[k, x, core], y2.at[k, x, core], y2_ss.at[k, i], y2_rs.at[k, i], rows_peer(*d))
                  for i, d in enumerate(y2_far)]
        for copy in copies:
            copy.wait_recv()
        q = jnp.concatenate(
            [(((y2[k, 0, c].astype(F32) + y2[k, 1, c].astype(F32)) + y2[k, 2, c].astype(F32)) + y2[k, 3, c].astype(F32)).astype(BF16)
             for c in range(2)], axis=0)

    gc[params] = gram(q)
    copies = []
    for dz, dy in yz_far:
        i = dz * NY + dy - 1
        copies.append(send(gc.at[params], gc.at[params], gc_ss.at[i], gc_rs.at[i], yz_peer(dz, dy)))
    for copy in copies:
        copy.wait_recv()
    total = gc[0]
    for i in range(1, NY * NZ):
        total = total + gc[i]
    out[...] = apply(split_inverse(total), q).astype(BF16)
    for copy in pending:
        copy.wait_send()


def local(jacobian, pattern, row_class, class_weight, probes):
    nrows, ncols = jacobian.shape
    k, n = ITERS, NY * NZ
    vmem, dma = pltpu.VMEM, pltpu.SemaphoreType.DMA
    return pl.pallas_call(
        kernel,
        out_shape=jax.ShapeDtypeStruct(probes.shape, BF16),
        in_specs=[
            pl.BlockSpec(memory_space=pltpu.SMEM),
            pl.BlockSpec(memory_space=pltpu.SMEM),
            pl.BlockSpec(memory_space=pl.ANY),
            pl.BlockSpec(memory_space=pltpu.VMEM),
            pl.BlockSpec(memory_space=pltpu.VMEM),
        ],
        out_specs=pl.BlockSpec(memory_space=pltpu.VMEM),
        scratch_shapes=[
            vmem((nrows, ncols), BF16), vmem((NZ, 1, nrows // NZ), F32), vmem((nrows // 128, 128), F32),
            vmem((128, ncols), BF16), vmem((2, 16, ncols), F32), vmem((NY, 32, BLOCK), F32),
            vmem((k, NZ, NY, 32, BLOCK), BF16), vmem((k, n - 1, 32, BLOCK), BF16), vmem((k, n, 32, BLOCK), BF16),
            vmem((k - 1, NY, 8, 128), F32), vmem((k - 1, NZ, 8, 128), F32), vmem((n, 8, 128), F32),
            vmem((k, 16, ncols), BF16), vmem((k, 4, 16, ncols), BF16), vmem((k, NX, 2, 16, ncols), BF16),
            dma((NZ,)),
            dma((k, n - 1)), dma((k, n - 1)), dma((k, n - 1)), dma((k, n - 1)),
            dma((k - 1, 3)), dma((k - 1, 3)), dma((k - 1, 3)), dma((k - 1, 3)), dma((n - 1,)), dma((n - 1,)),
            dma((k, 3)), dma((k, 3)), dma((k, 7)), dma((k, 7)),
        ],
        compiler_params=pltpu.CompilerParams(collective_id=0, has_side_effects=True),
    )(pattern, class_weight, jacobian, row_class.reshape(-1, 128), probes)


def solution(mesh):
    placed = (P("rows", "params"), P("rows", "params"), P("rows"), P(), P(None, "params"))
    return jax.shard_map(
        local, mesh=mesh, in_specs=placed, out_specs=P(None, "params"), check_vma=False
    )
```

```python
import functools
import math

import jax
import jax.numpy as jnp
from jax import lax
from jax.experimental import pallas as pl
from jax.experimental.pallas import tpu as pltpu
from jax.sharding import PartitionSpec as P

P_SIZE = 12288
BLOCK = 128
ITERS = 4
NY, NZ, NX = 4, 4, 4
MESH = pl.DeviceIdType.MESH
BF16, F32 = jnp.bfloat16, jnp.float32


def dot_t(a, b):
    return lax.dot_general(a, b, (((1,), (1,)), ((), ())), preferred_element_type=F32)


def dot(a, b):
    return jnp.dot(a, b, preferred_element_type=F32)


def pack_gram(g):
    return g[0:8] + pltpu.roll(g[8:16], 32, 1) + pltpu.roll(g[16:24], 64, 1) + pltpu.roll(g[24:32], 96, 1)


def scaled_inverse(gp, scale):
    a = jnp.concatenate([gp, pltpu.roll(gp, 96, 1), pltpu.roll(gp, 64, 1), pltpu.roll(gp, 32, 1)], axis=0)
    n = a.shape[0]
    row = lax.broadcasted_iota(jnp.int32, a.shape, 0)
    lane = lax.broadcasted_iota(jnp.int32, a.shape, 1)
    b = jnp.where(lane < n, a, jnp.where(lane - n == row, 1.0, 0.0))
    for j in range(n - 1):
        factor = b[:, j : j + 1] * (1.0 / b[j : j + 1, j : j + 1])
        b = jnp.where(row > j, b - factor * b[j : j + 1, :], b)
    diag = jnp.sum(jnp.where(lane == row, b, 0.0), axis=1, keepdims=True)
    inv = pltpu.roll(b, 128 - n, 1) * (lax.rsqrt(diag) * scale)
    return inv[:, :n]


def kernel(pattern_h, class_weight_h, jac, row_class_h, probes_h, out, pattern, class_weight, row_class, probes, m, w, w16, qpad, yacc, zown,
           za_s, za_r, zc, ga, gb, gc, ys, y1, y2, load_sem, in_sem,
           za_ss, za_rs, zc_ss, zc_rs, ga_ss, ga_rs, gb_ss, gb_rs, gc_ss, gc_rs,
           y1_ss, y1_rs, y2_ss, y2_rs):
    rows, params = lax.axis_index("rows"), lax.axis_index("params")
    y, zl = lax.rem(params, NY), lax.div(params, NY)
    core, zh, x = lax.rem(rows, 2), lax.rem(lax.div(rows, 2), 2), lax.div(rows, 4)
    group = m.shape[0] // NZ
    per = group // BLOCK
    scale = math.sqrt(P_SIZE)
    pending = []

    def yz_peer(dz, dy):
        return {"params": lax.rem(zl + dz, NZ) * NY + lax.rem(y + dy, NY)}

    def rows_peer(dx, dz, dc):
        return {"rows": lax.rem(x + dx, NX) * 4 + lax.rem(zh + dz, 2) * 2 + lax.rem(core + dc, 2)}

    def device(tz, ty):
        return {"params": tz * NY + ty}

    low = 1 - lax.div(zl, 2)
    z_order = [3 * low, 1 + low, zl + 1 - 2 * lax.rem(zl, 2), zl]
    y_order = [lax.rem(y + dy, NY) for dy in (2, 1, 3, 0)]
    others = [(tz, ty) for tz in z_order for ty in y_order][:-1]
    y1_far = [(0, 1, 1), (0, 1, 0), (0, 0, 1)]
    y2_far = [(2, 0, 1), (2, 0, 0), (1, 0, 1), (3, 0, 1), (1, 0, 0), (3, 0, 0), (0, 0, 1)]

    def send(src, dst, ssem, rsem, peer):
        copy = pltpu.make_async_remote_copy(
            src_ref=src, dst_ref=dst, send_sem=ssem, recv_sem=rsem, device_id=peer, device_id_type=MESH)
        copy.start()
        pending.append(copy)
        return copy

    inputs = [pltpu.make_async_copy(src, dst, in_sem.at[i]) for i, (src, dst) in enumerate(
        ((pattern_h, pattern), (probes_h, probes), (row_class_h, row_class), (class_weight_h, class_weight)))]
    loads = []
    for i, c in enumerate(z_order):
        at = pl.ds(pl.multiple_of(c * group, group), group)
        loads.append(pltpu.make_async_copy(jac.at[at, :], m.at[at, :], load_sem.at[i]))
    inputs[0].start()
    inputs[1].start()
    loads[0].start()
    inputs[2].start()
    inputs[3].start()
    for copy in loads[1:]:
        copy.start()

    barrier = pltpu.get_barrier_semaphore()
    friends = [device(*t) for t in others] + [rows_peer(*d) for d in y1_far + y2_far[:-1]]
    for peer in friends:
        pl.semaphore_signal(barrier, inc=1, device_id=peer, device_id_type=MESH)

    def prepare(i):
        loads[i].wait()
        c = z_order[i]
        for r in range(per):
            for j in range(pattern.shape[0]):
                keep = jnp.full((BLOCK, BLOCK), pattern[j, c * per + r].astype(F32)).astype(BF16)
                at = (pl.ds(pl.multiple_of(c * group + r * BLOCK, BLOCK), BLOCK), pl.ds(j * BLOCK, BLOCK))
                m[at] = m[at] * keep

    def weigh():
        inputs[2].wait()
        inputs[3].wait()
        classes = row_class[...]
        weight = jnp.zeros(classes.shape, F32)
        for c in range(class_weight.shape[0]):
            weight = jnp.where(classes == c, class_weight[c], weight)
        w16[...] = weight
        for c in range(NZ):
            for i in range(per):
                w[c, :, i * BLOCK : (i + 1) * BLOCK] = w16[c * per + i : c * per + i + 1, :]

    def rows_of(c):
        return m[pl.ds(pl.multiple_of(c * group, group), group), :]

    def raw_z(k, q, n):
        part = dot_t(q, rows_of(z_order[n]))
        for i in range(NY):
            block = part[:, i * BLOCK : (i + 1) * BLOCK]
            za_s[k, n, i] = block.astype(BF16)
            if n == NZ - 1:
                zown[i] = block

    def scatter_z(k, n):
        for i in range(n * NY, min((n + 1) * NY, len(others))):
            tz, ty = others[i]
            send(za_s.at[k, n, ty], za_r.at[k, params], za_ss.at[k, i], za_rs.at[k, params], device(tz, ty))

    def await_from(buf, sem, k, t):
        p = t[0] * NY + t[1]
        pltpu.make_async_remote_copy(
            src_ref=buf.at[k, p], dst_ref=buf.at[k, p], send_sem=sem.at[k, p], recv_sem=sem.at[k, p],
            device_id=device(*t), device_id_type=MESH).wait_recv()
        return p

    def gram(q):
        qpad[0:32, :] = q
        return pack_gram(dot_t(q, qpad[...]))

    def scatter_gram(k, q):
        ga[k, y] = gram(q)
        return [send(ga.at[k, y], ga.at[k, y], ga_ss.at[k, d - 1], ga_rs.at[k, d - 1], yz_peer(0, d))
                for d in (2, 1, 3)]

    def forward_gram(k, copies):
        for copy in copies:
            copy.wait_recv()
        gb[k, zl] = ((ga[k, 0] + ga[k, 1]) + ga[k, 2]) + ga[k, 3]
        return [send(gb.at[k, zl], gb.at[k, zl], gb_ss.at[k, d - 1], gb_rs.at[k, d - 1], yz_peer(d, 0))
                for d in (2, 3, 1)]

    def split_inverse(g):
        inv = scaled_inverse(g, scale)
        high = inv.astype(BF16)
        low = (inv - high.astype(F32)).astype(BF16)
        return jnp.concatenate([high, low], axis=0)

    def apply(inv2, v):
        u = dot(inv2, v)
        return u[:32] + u[32:]

    inputs[1].wait()
    inputs[0].wait()
    q = probes[...]
    for k in range(ITERS):
        for n in range(NZ):
            if k == 0:
                prepare(n)
            raw_z(k, q, n)
            if k == 0 and n == 0:
                pl.semaphore_wait(barrier, len(friends))
            scatter_z(k, n)
            if k > 0 and n == 0:
                g_copies = scatter_gram(k - 1, q)
        if k == 0:
            weigh()
            qpad[...] = jnp.zeros_like(qpad)
        else:
            g_copies = forward_gram(k - 1, g_copies)
        total = zown[y]
        for t in reversed(others):
            total = total + za_r[k, await_from(za_r, za_rs, k, t)].astype(F32)
        zc[k, params] = total.astype(BF16)
        for i, t in enumerate(others):
            send(zc.at[k, params], zc.at[k, params], zc_ss.at[k, i], zc_rs.at[k, params], device(*t))
        if k > 0:
            for copy in g_copies:
                copy.wait_recv()
            inv2 = split_inverse(((gb[k - 1, 0] + gb[k - 1, 1]) + gb[k - 1, 2]) + gb[k - 1, 3])
        acc = None
        for n in reversed(range(NZ)):
            c = z_order[n]
            for t in others[n * NY : (n + 1) * NY]:
                await_from(zc, zc_rs, k, t)
            z = jnp.concatenate([zc[k, c * NY + i] for i in range(NY)], axis=1)
            z = z.astype(F32) if k == 0 else apply(inv2, z)
            v = (z * w[c]).astype(BF16)
            part = dot(v, rows_of(c))
            acc = part if acc is None else acc + part
        yacc[0] = acc[:16]
        yacc[1] = acc[16:]
        mine = zh * 2 + core
        ys[k] = yacc[1 - core].astype(BF16)
        y1[k, mine] = yacc[core].astype(BF16)
        copies = []
        for i, (dx, dz, dc) in enumerate(y1_far):
            src = ys.at[k] if dc else y1.at[k, mine]
            copies.append(send(src, y1.at[k, mine], y1_ss.at[k, i], y1_rs.at[k, i], rows_peer(dx, dz, dc)))
        for copy in copies:
            copy.wait_recv()
        total = ((y1[k, 0].astype(F32) + y1[k, 1].astype(F32)) + y1[k, 2].astype(F32)) + y1[k, 3].astype(F32)
        y2[k, x, core] = total.astype(BF16)
        copies = [send(y2.at[k, x, core], y2.at[k, x, core], y2_ss.at[k, i], y2_rs.at[k, i], rows_peer(*d))
                  for i, d in enumerate(y2_far)]
        for copy in copies:
            copy.wait_recv()
        q = jnp.concatenate(
            [(((y2[k, 0, c].astype(F32) + y2[k, 1, c].astype(F32)) + y2[k, 2, c].astype(F32)) + y2[k, 3, c].astype(F32)).astype(BF16)
             for c in range(2)], axis=0)

    gc[0, params] = gram(q)
    for i, t in enumerate(others):
        send(gc.at[0, params], gc.at[0, params], gc_ss.at[i], gc_rs.at[0, params], device(*t))
    for t in others:
        await_from(gc, gc_rs, 0, t)
    total = gc[0, 0]
    for i in range(1, NY * NZ):
        total = total + gc[0, i]
    out[...] = apply(split_inverse(total), q).astype(BF16)
    for copy in pending:
        copy.wait_send()


def local(jacobian, pattern, row_class, class_weight, probes):
    nrows, ncols = jacobian.shape
    k, n = ITERS, NY * NZ
    vmem, dma = pltpu.VMEM, pltpu.SemaphoreType.DMA
    return pl.pallas_call(
        kernel,
        out_shape=jax.ShapeDtypeStruct(probes.shape, BF16),
        in_specs=[pl.BlockSpec(memory_space=pl.ANY)] * 5,
        out_specs=pl.BlockSpec(memory_space=pltpu.VMEM),
        scratch_shapes=[
            pltpu.SMEM(pattern.shape[::-1], jnp.int32), pltpu.SMEM(class_weight.shape, F32),
            vmem((nrows // 128, 128), jnp.int32), vmem(probes.shape, BF16),
            vmem((nrows, ncols), BF16), vmem((NZ, 1, nrows // NZ), F32), vmem((nrows // 128, 128), F32),
            vmem((128, ncols), BF16), vmem((2, 16, ncols), F32), vmem((NY, 32, BLOCK), F32),
            vmem((k, NZ, NY, 32, BLOCK), BF16), vmem((k, n, 32, BLOCK), BF16), vmem((k, n, 32, BLOCK), BF16),
            vmem((k - 1, NY, 8, 128), F32), vmem((k - 1, NZ, 8, 128), F32), vmem((1, n, 8, 128), F32),
            vmem((k, 16, ncols), BF16), vmem((k, 4, 16, ncols), BF16), vmem((k, NX, 2, 16, ncols), BF16),
            dma((NZ,)), dma((4,)),
            dma((k, n - 1)), dma((k, n)), dma((k, n - 1)), dma((k, n)),
            dma((k - 1, 3)), dma((k - 1, 3)), dma((k - 1, 3)), dma((k - 1, 3)), dma((n - 1,)), dma((1, n)),
            dma((k, 3)), dma((k, 3)), dma((k, 7)), dma((k, 7)),
        ],
        compiler_params=pltpu.CompilerParams(collective_id=0, has_side_effects=True),
    )(pattern.T, class_weight, jacobian, row_class.reshape(-1, 128), probes)


def solution(mesh):
    placed = (P("rows", "params"), P("rows", "params"), P("rows"), P(), P(None, "params"))
    return jax.shard_map(
        local, mesh=mesh, in_specs=placed, out_specs=P(None, "params"), check_vma=False
    )
```

```python
import functools
import math

import jax
import jax.numpy as jnp
from jax import lax
from jax.experimental import pallas as pl
from jax.experimental.pallas import tpu as pltpu
from jax.sharding import PartitionSpec as P

P_SIZE = 12288
BLOCK = 128
ITERS = 4
NY, NZ, NX = 4, 4, 4
MESH = pl.DeviceIdType.MESH
BF16, F32 = jnp.bfloat16, jnp.float32


def dot_t(a, b):
    return lax.dot_general(a, b, (((1,), (1,)), ((), ())), preferred_element_type=F32)


def dot(a, b):
    return jnp.dot(a, b, preferred_element_type=F32)


def add_all(terms):
    total = terms[0].astype(F32)
    for term in terms[1:]:
        total = total + term.astype(F32)
    return total


def pack_gram(g):
    return g[0:8] + pltpu.roll(g[8:16], 32, 1) + pltpu.roll(g[16:24], 64, 1) + pltpu.roll(g[24:32], 96, 1)


def scaled_inverse(gp, scale):
    a = jnp.concatenate([gp, pltpu.roll(gp, 96, 1), pltpu.roll(gp, 64, 1), pltpu.roll(gp, 32, 1)], axis=0)
    n = a.shape[0]
    row = lax.broadcasted_iota(jnp.int32, a.shape, 0)
    lane = lax.broadcasted_iota(jnp.int32, a.shape, 1)
    b = jnp.where(lane < n, a, jnp.where(lane - n == row, 1.0, 0.0))
    for j in range(n - 1):
        factor = b[:, j : j + 1] * (1.0 / b[j : j + 1, j : j + 1])
        b = jnp.where(row > j, b - factor * b[j : j + 1, :], b)
    diag = jnp.sum(jnp.where(lane == row, b, 0.0), axis=1, keepdims=True)
    inv = pltpu.roll(b, 128 - n, 1) * (lax.rsqrt(diag) * scale)
    return inv[:, :n]


def kernel(pattern_h, class_weight_h, jac, row_class_h, probes_h, out, pattern, class_weight, row_class, probes, m, w, w16, qpad, zown,
           za_s, za_r, zc, ga, gb, gc, yp, a1, a2, b1, b2, load_sem, in_sem,
           za_ss, za_rs, zc_ss, zc_rs, ga_ss, ga_rs, gb_ss, gb_rs, gc_ss, gc_rs,
           a1_ss, a1_rs, a2_ss, a2_rs, b1_ss, b1_rs, b2_ss, b2_rs):
    rows, params = lax.axis_index("rows"), lax.axis_index("params")
    y, zl = lax.rem(params, NY), lax.div(params, NY)
    core, zh, x = lax.rem(rows, 2), lax.rem(lax.div(rows, 2), 2), lax.div(rows, 4)
    group = m.shape[0] // NZ
    per = group // BLOCK
    half = m.shape[1] // 2
    scale = math.sqrt(P_SIZE)
    pending = []

    def yz_peer(dz, dy):
        return {"params": lax.rem(zl + dz, NZ) * NY + lax.rem(y + dy, NY)}

    def rows_peer(dx, dz, dc):
        return {"rows": lax.rem(x + dx, NX) * 4 + lax.rem(zh + dz, 2) * 2 + lax.rem(core + dc, 2)}

    def device(tz, ty):
        return {"params": tz * NY + ty}

    low = 1 - lax.div(zl, 2)
    z_order = [3 * low, 1 + low, zl + 1 - 2 * lax.rem(zl, 2), zl]
    y_order = [lax.rem(y + dy, NY) for dy in (2, 1, 3, 0)]
    others = [(tz, ty) for tz in z_order for ty in y_order][:-1]
    z_far = [(0, 1, 1), (0, 1, 0), (0, 0, 1)]
    x_far = [(2, 0, 1), (2, 0, 0), (1, 0, 1), (3, 0, 1), (1, 0, 0), (3, 0, 0), (0, 0, 1)]

    def send(src, dst, ssem, rsem, peer):
        copy = pltpu.make_async_remote_copy(
            src_ref=src, dst_ref=dst, send_sem=ssem, recv_sem=rsem, device_id=peer, device_id_type=MESH)
        copy.start()
        pending.append(copy)
        return copy

    inputs = [pltpu.make_async_copy(src, dst, in_sem.at[i]) for i, (src, dst) in enumerate(
        ((pattern_h, pattern), (probes_h, probes), (row_class_h, row_class), (class_weight_h, class_weight)))]
    loads = []
    for i, c in enumerate(z_order):
        at = pl.ds(pl.multiple_of(c * group, group), group)
        loads.append(pltpu.make_async_copy(jac.at[at, :], m.at[at, :], load_sem.at[i]))
    inputs[0].start()
    inputs[1].start()
    loads[0].start()
    inputs[2].start()
    inputs[3].start()
    for copy in loads[1:]:
        copy.start()

    barrier = pltpu.get_barrier_semaphore()
    friends = [device(*t) for t in others] + [rows_peer(*d) for d in z_far + x_far[:-1]]
    for peer in friends:
        pl.semaphore_signal(barrier, inc=1, device_id=peer, device_id_type=MESH)

    def prepare(i):
        loads[i].wait()
        c = z_order[i]
        for r in range(per):
            for j in range(pattern.shape[0]):
                keep = jnp.full((BLOCK, BLOCK), pattern[j, c * per + r].astype(F32)).astype(BF16)
                at = (pl.ds(pl.multiple_of(c * group + r * BLOCK, BLOCK), BLOCK), pl.ds(j * BLOCK, BLOCK))
                m[at] = m[at] * keep

    def weigh():
        inputs[2].wait()
        inputs[3].wait()
        classes = row_class[...]
        weight = jnp.zeros(classes.shape, F32)
        for c in range(class_weight.shape[0]):
            weight = jnp.where(classes == c, class_weight[c], weight)
        w16[...] = weight
        for c in range(NZ):
            for i in range(per):
                w[c, :, i * BLOCK : (i + 1) * BLOCK] = w16[c * per + i : c * per + i + 1, :]

    def rows_of(c):
        return m[pl.ds(pl.multiple_of(c * group, group), group), :]

    def raw_z(k, q, n):
        part = dot_t(q, rows_of(z_order[n]))
        for i in range(NY):
            block = part[:, i * BLOCK : (i + 1) * BLOCK]
            za_s[k, n, i] = block.astype(BF16)
            if n == NZ - 1:
                zown[i] = block

    def scatter_z(k, n):
        for i in range(n * NY, min((n + 1) * NY, len(others))):
            tz, ty = others[i]
            send(za_s.at[k, n, ty], za_r.at[k, params], za_ss.at[k, i], za_rs.at[k, params], device(tz, ty))

    def await_from(buf, sem, k, t):
        p = t[0] * NY + t[1]
        pltpu.make_async_remote_copy(
            src_ref=buf.at[k, p], dst_ref=buf.at[k, p], send_sem=sem.at[k, p], recv_sem=sem.at[k, p],
            device_id=device(*t), device_id_type=MESH).wait_recv()
        return p

    def gram(q):
        qpad[0:32, :] = q
        return pack_gram(dot_t(q, qpad[...]))

    def scatter_gram(k, q):
        ga[k, y] = gram(q)
        return [send(ga.at[k, y], ga.at[k, y], ga_ss.at[k, d - 1], ga_rs.at[k, d - 1], yz_peer(0, d))
                for d in (2, 1, 3)]

    def forward_gram(k, copies):
        for copy in copies:
            copy.wait_recv()
        gb[k, zl] = ((ga[k, 0] + ga[k, 1]) + ga[k, 2]) + ga[k, 3]
        return [send(gb.at[k, zl], gb.at[k, zl], gb_ss.at[k, d - 1], gb_rs.at[k, d - 1], yz_peer(d, 0))
                for d in (2, 3, 1)]

    def split_inverse(g):
        inv = scaled_inverse(g, scale)
        high = inv.astype(BF16)
        low = (inv - high.astype(F32)).astype(BF16)
        return jnp.concatenate([high, low], axis=0)

    def apply(inv2, v):
        u = dot(inv2, v)
        return u[:32] + u[32:]

    inputs[1].wait()
    inputs[0].wait()
    q = probes[...]
    for k in range(ITERS):
        for n in range(NZ):
            if k == 0:
                prepare(n)
            raw_z(k, q, n)
            if k == 0 and n == 0:
                pl.semaphore_wait(barrier, len(friends))
            scatter_z(k, n)
            if k > 0 and n == 0:
                g_copies = scatter_gram(k - 1, q)
        if k == 0:
            weigh()
            qpad[...] = jnp.zeros_like(qpad)
        else:
            g_copies = forward_gram(k - 1, g_copies)
        total = zown[y]
        for t in reversed(others):
            total = total + za_r[k, await_from(za_r, za_rs, k, t)].astype(F32)
        zc[k, params] = total.astype(BF16)
        for i, t in enumerate(others):
            send(zc.at[k, params], zc.at[k, params], zc_ss.at[k, i], zc_rs.at[k, params], device(*t))
        if k > 0:
            for copy in g_copies:
                copy.wait_recv()
            inv2 = split_inverse(((gb[k - 1, 0] + gb[k - 1, 1]) + gb[k - 1, 2]) + gb[k - 1, 3])
        acc = None
        for n in reversed(range(NZ)):
            c = z_order[n]
            for t in others[n * NY : (n + 1) * NY]:
                await_from(zc, zc_rs, k, t)
            z = jnp.concatenate([zc[k, c * NY + i] for i in range(NY)], axis=1)
            z = z.astype(F32) if k == 0 else apply(inv2, z)
            v = (z * w[c]).astype(BF16)
            part = dot(v, rows_of(c))
            acc = part if acc is None else acc + part
        for h in range(2):
            for f in range(2):
                yp[k, h, f] = acc[16 * h : 16 * h + 16, half * f : half * f + half].astype(BF16)
        za, xa = zh * 2 + core, x * 2 + core
        a1[k, za] = yp[k, core, 0]
        b1[k, xa] = yp[k, core, 1]

        def exchange(far, source, dst, ss, rs):
            return [send(source(d[2]), dst, ss.at[k, i], rs.at[k, i], rows_peer(*d)) for i, d in enumerate(far)]

        a_copies = exchange(z_far, lambda dc: yp.at[k, lax.rem(core + dc, 2), 0], a1.at[k, za], a1_ss, a1_rs)
        b_copies = exchange(x_far, lambda dc: yp.at[k, lax.rem(core + dc, 2), 1], b1.at[k, xa], b1_ss, b1_rs)
        for copy in b_copies:
            copy.wait_recv()
        b2[k, za] = add_all([b1[k, i] for i in range(2 * NX)]).astype(BF16)
        b_copies = exchange(z_far, lambda dc: b2.at[k, za], b2.at[k, za], b2_ss, b2_rs)
        for copy in a_copies:
            copy.wait_recv()
        a2[k, xa] = add_all([a1[k, i] for i in range(4)]).astype(BF16)
        a_copies = exchange(x_far, lambda dc: a2.at[k, xa], a2.at[k, xa], a2_ss, a2_rs)
        for copy in a_copies + b_copies:
            copy.wait_recv()
        q = jnp.concatenate([
            jnp.concatenate([
                add_all([a2[k, i * 2 + c] for i in range(NX)]).astype(BF16),
                add_all([b2[k, i * 2 + c] for i in range(2)]).astype(BF16)], axis=1)
            for c in range(2)], axis=0)

    gc[0, params] = gram(q)
    for i, t in enumerate(others):
        send(gc.at[0, params], gc.at[0, params], gc_ss.at[i], gc_rs.at[0, params], device(*t))
    for t in others:
        await_from(gc, gc_rs, 0, t)
    total = gc[0, 0]
    for i in range(1, NY * NZ):
        total = total + gc[0, i]
    out[...] = apply(split_inverse(total), q).astype(BF16)
    for copy in pending:
        copy.wait_send()


def local(jacobian, pattern, row_class, class_weight, probes):
    nrows, ncols = jacobian.shape
    k, n, half = ITERS, NY * NZ, ncols // 2
    vmem, dma = pltpu.VMEM, pltpu.SemaphoreType.DMA
    return pl.pallas_call(
        kernel,
        out_shape=jax.ShapeDtypeStruct(probes.shape, BF16),
        in_specs=[pl.BlockSpec(memory_space=pl.ANY)] * 5,
        out_specs=pl.BlockSpec(memory_space=pltpu.VMEM),
        scratch_shapes=[
            pltpu.SMEM(pattern.shape[::-1], jnp.int32), pltpu.SMEM(class_weight.shape, F32),
            vmem((nrows // 128, 128), jnp.int32), vmem(probes.shape, BF16),
            vmem((nrows, ncols), BF16), vmem((NZ, 1, nrows // NZ), F32), vmem((nrows // 128, 128), F32),
            vmem((128, ncols), BF16), vmem((NY, 32, BLOCK), F32),
            vmem((k, NZ, NY, 32, BLOCK), BF16), vmem((k, n, 32, BLOCK), BF16), vmem((k, n, 32, BLOCK), BF16),
            vmem((k - 1, NY, 8, 128), F32), vmem((k - 1, NZ, 8, 128), F32), vmem((1, n, 8, 128), F32),
            vmem((k, 2, 2, 16, half), BF16), vmem((k, 4, 16, half), BF16), vmem((k, 2 * NX, 16, half), BF16),
            vmem((k, 2 * NX, 16, half), BF16), vmem((k, 4, 16, half), BF16),
            dma((NZ,)), dma((4,)),
            dma((k, n - 1)), dma((k, n)), dma((k, n - 1)), dma((k, n)),
            dma((k - 1, 3)), dma((k - 1, 3)), dma((k - 1, 3)), dma((k - 1, 3)), dma((n - 1,)), dma((1, n)),
            dma((k, 3)), dma((k, 3)), dma((k, 7)), dma((k, 7)), dma((k, 7)), dma((k, 7)), dma((k, 3)), dma((k, 3)),
        ],
        compiler_params=pltpu.CompilerParams(collective_id=0, has_side_effects=True, vmem_limit_bytes=32 * 2**20),
    )(*(pltpu.with_memory_space_constraint(a, pltpu.HBM)
        for a in (pattern.T, class_weight, jacobian, row_class.reshape(-1, 128), probes)))


def solution(mesh):
    placed = (P("rows", "params"), P("rows", "params"), P("rows"), P(), P(None, "params"))
    return jax.shard_map(
        local, mesh=mesh, in_specs=placed, out_specs=P(None, "params"), check_vma=False
    )
```

```python
import functools
import math

import jax
import jax.numpy as jnp
from jax import lax
from jax.experimental import pallas as pl
from jax.experimental.pallas import tpu as pltpu
from jax.sharding import PartitionSpec as P

P_SIZE = 12288
BLOCK = 128
ITERS = 4
NY, NZ, NX = 4, 4, 4
MESH = pl.DeviceIdType.MESH
BF16, F32 = jnp.bfloat16, jnp.float32


def dot_t(a, b):
    return lax.dot_general(a, b, (((1,), (1,)), ((), ())), preferred_element_type=F32)


def dot(a, b):
    return jnp.dot(a, b, preferred_element_type=F32)


def add_all(terms):
    total = terms[0].astype(F32)
    for term in terms[1:]:
        total = total + term.astype(F32)
    return total


def pack_gram(g):
    return g[0:8] + pltpu.roll(g[8:16], 32, 1) + pltpu.roll(g[16:24], 64, 1) + pltpu.roll(g[24:32], 96, 1)


def scaled_inverse(gp, scale):
    tile = gp.shape
    row = lax.broadcasted_iota(jnp.int32, tile, 0)
    lane = lax.broadcasted_iota(jnp.int32, tile, 1)
    nb, n = 4, 32
    b = []
    for i in range(nb):
        a = pltpu.roll(gp, 128 - 32 * i, 1) if i else gp
        b.append(jnp.where(lane < n, a, jnp.where(lane - n == row + 8 * i, 1.0, 0.0)))

    def spread(v):
        return jnp.broadcast_to(v, tile)

    for g in range(nb):
        col = {i: [spread(b[i][:, 8 * g + k : 8 * g + k + 1]) for k in range(8)] for i in range(g, nb)}
        r = [spread(b[g][m : m + 1, :]) for m in range(8)]
        a = {(m, k): spread(col[g][k][m : m + 1, :]) for m in range(8) for k in range(m + 1)}
        for k in range(8):
            inv = 1.0 / a[k, k]
            for i in range(g + 1, nb):
                factor = col[i][k] * inv
                b[i] = b[i] - factor * r[k]
                for m in range(k + 1, 8):
                    col[i][m] = col[i][m] - factor * a[m, k]
            for m in range(k + 1, 8):
                factor = a[m, k] * inv
                r[m] = r[m] - factor * r[k]
                for l in range(k + 1, m + 1):
                    a[m, l] = a[m, l] - factor * a[l, k]
        for m in range(8):
            b[g] = jnp.where(row == m, r[m], b[g])
    out = []
    for i in range(nb):
        diag = jnp.sum(jnp.where(lane == row + 8 * i, b[i], 0.0), axis=1, keepdims=True)
        out.append(pltpu.roll(b[i], 128 - n, 1) * (lax.rsqrt(diag) * scale))
    return jnp.concatenate(out, axis=0)[:, :n]


def kernel(pattern_h, class_weight_h, jac, row_class_h, probes_h, out, pattern, class_weight, row_class, probes, m, w, w16, qpad, zown,
           za_s, za_r, zc, ga, gb, gc, yp, a1, a2, b1, b2, load_sem, in_sem,
           za_ss, za_rs, zc_ss, zc_rs, ga_ss, ga_rs, gb_ss, gb_rs, gc_ss, gc_rs,
           a1_ss, a1_rs, a2_ss, a2_rs, b1_ss, b1_rs, b2_ss, b2_rs):
    rows, params = lax.axis_index("rows"), lax.axis_index("params")
    y, zl = lax.rem(params, NY), lax.div(params, NY)
    core, zh, x = lax.rem(rows, 2), lax.rem(lax.div(rows, 2), 2), lax.div(rows, 4)
    group = m.shape[0] // NZ
    per = group // BLOCK
    half = m.shape[1] // 2
    scale = math.sqrt(P_SIZE)
    pending = []

    def yz_peer(dz, dy):
        return {"params": lax.rem(zl + dz, NZ) * NY + lax.rem(y + dy, NY)}

    def rows_peer(dx, dz, dc):
        return {"rows": lax.rem(x + dx, NX) * 4 + lax.rem(zh + dz, 2) * 2 + lax.rem(core + dc, 2)}

    def device(tz, ty):
        return {"params": tz * NY + ty}

    low = 1 - lax.div(zl, 2)
    z_order = [3 * low, 1 + low, zl + 1 - 2 * lax.rem(zl, 2), zl]
    y_order = [lax.rem(y + dy, NY) for dy in (2, 1, 3, 0)]
    others = [(tz, ty) for tz in z_order for ty in y_order][:-1]
    z_far = [(0, 1, 1), (0, 1, 0), (0, 0, 1)]
    x_far = [(2, 0, 1), (2, 0, 0), (1, 0, 1), (3, 0, 1), (1, 0, 0), (3, 0, 0), (0, 0, 1)]

    def send(src, dst, ssem, rsem, peer):
        copy = pltpu.make_async_remote_copy(
            src_ref=src, dst_ref=dst, send_sem=ssem, recv_sem=rsem, device_id=peer, device_id_type=MESH)
        copy.start()
        pending.append(copy)
        return copy

    inputs = [pltpu.make_async_copy(src, dst, in_sem.at[i]) for i, (src, dst) in enumerate(
        ((pattern_h, pattern), (probes_h, probes), (row_class_h, row_class), (class_weight_h, class_weight)))]
    loads = []
    for i, c in enumerate(z_order):
        at = pl.ds(pl.multiple_of(c * group, group), group)
        loads.append(pltpu.make_async_copy(jac.at[at, :], m.at[at, :], load_sem.at[i]))
    inputs[0].start()
    inputs[1].start()
    loads[0].start()
    inputs[2].start()
    inputs[3].start()
    for copy in loads[1:]:
        copy.start()

    barrier = pltpu.get_barrier_semaphore()
    friends = [device(*t) for t in others] + [rows_peer(*d) for d in z_far + x_far[:-1]]
    for peer in friends:
        pl.semaphore_signal(barrier, inc=1, device_id=peer, device_id_type=MESH)

    def prepare(i):
        loads[i].wait()
        c = z_order[i]
        for r in range(per):
            for j in range(pattern.shape[0]):
                keep = jnp.full((BLOCK, BLOCK), pattern[j, c * per + r].astype(F32)).astype(BF16)
                at = (pl.ds(pl.multiple_of(c * group + r * BLOCK, BLOCK), BLOCK), pl.ds(j * BLOCK, BLOCK))
                m[at] = m[at] * keep

    def weigh():
        inputs[2].wait()
        inputs[3].wait()
        classes = row_class[...]
        weight = jnp.zeros(classes.shape, F32)
        for c in range(class_weight.shape[0]):
            weight = jnp.where(classes == c, class_weight[c], weight)
        w16[...] = weight
        for c in range(NZ):
            for i in range(per):
                w[c, :, i * BLOCK : (i + 1) * BLOCK] = w16[c * per + i : c * per + i + 1, :]

    def rows_of(c):
        return m[pl.ds(pl.multiple_of(c * group, group), group), :]

    def raw_z(k, q, n):
        part = dot_t(q, rows_of(z_order[n]))
        for i in range(NY):
            block = part[:, i * BLOCK : (i + 1) * BLOCK]
            za_s[k, n, i] = block.astype(BF16)
            if n == NZ - 1:
                zown[i] = block

    def scatter_z(k, n):
        for i in range(n * NY, min((n + 1) * NY, len(others))):
            tz, ty = others[i]
            send(za_s.at[k, n, ty], za_r.at[k, params], za_ss.at[k, i], za_rs.at[k, params], device(tz, ty))

    def await_from(buf, sem, k, t):
        p = t[0] * NY + t[1]
        pltpu.make_async_remote_copy(
            src_ref=buf.at[k, p], dst_ref=buf.at[k, p], send_sem=sem.at[k, p], recv_sem=sem.at[k, p],
            device_id=device(*t), device_id_type=MESH).wait_recv()
        return p

    def gram(q):
        qpad[0:32, :] = q
        return pack_gram(dot_t(q, qpad[...]))

    def scatter_gram(k, q):
        ga[k, y] = gram(q)
        return [send(ga.at[k, y], ga.at[k, y], ga_ss.at[k, d - 1], ga_rs.at[k, d - 1], yz_peer(0, d))
                for d in (2, 1, 3)]

    def forward_gram(k, copies):
        for copy in copies:
            copy.wait_recv()
        gb[k, zl] = ((ga[k, 0] + ga[k, 1]) + ga[k, 2]) + ga[k, 3]
        return [send(gb.at[k, zl], gb.at[k, zl], gb_ss.at[k, d - 1], gb_rs.at[k, d - 1], yz_peer(d, 0))
                for d in (2, 3, 1)]

    def split_inverse(g):
        inv = scaled_inverse(g, scale)
        high = inv.astype(BF16)
        low = (inv - high.astype(F32)).astype(BF16)
        return jnp.concatenate([high, low], axis=0)

    def apply(inv2, v):
        u = dot(inv2, v)
        return u[:32] + u[32:]

    inputs[1].wait()
    inputs[0].wait()
    q = probes[...]
    for k in range(ITERS):
        for n in range(NZ):
            if k == 0:
                prepare(n)
            raw_z(k, q, n)
            if k == 0 and n == 0:
                pl.semaphore_wait(barrier, len(friends))
            scatter_z(k, n)
            if k > 0 and n == 0:
                g_copies = scatter_gram(k - 1, q)
        if k == 0:
            weigh()
            qpad[...] = jnp.zeros_like(qpad)
        else:
            g_copies = forward_gram(k - 1, g_copies)
        total = zown[y]
        for t in reversed(others):
            total = total + za_r[k, await_from(za_r, za_rs, k, t)].astype(F32)
        zc[k, params] = total.astype(BF16)
        for i, t in enumerate(others):
            send(zc.at[k, params], zc.at[k, params], zc_ss.at[k, i], zc_rs.at[k, params], device(*t))
        if k > 0:
            for copy in g_copies:
                copy.wait_recv()
            inv2 = split_inverse(((gb[k - 1, 0] + gb[k - 1, 1]) + gb[k - 1, 2]) + gb[k - 1, 3])
        acc = None
        for n in reversed(range(NZ)):
            c = z_order[n]
            for t in others[n * NY : (n + 1) * NY]:
                await_from(zc, zc_rs, k, t)
            z = jnp.concatenate([zc[k, c * NY + i] for i in range(NY)], axis=1)
            z = z.astype(F32) if k == 0 else apply(inv2, z)
            v = (z * w[c]).astype(BF16)
            part = dot(v, rows_of(c))
            acc = part if acc is None else acc + part
        for h in range(2):
            for f in range(2):
                yp[k, h, f] = acc[16 * h : 16 * h + 16, half * f : half * f + half].astype(BF16)
        za, xa = zh * 2 + core, x * 2 + core
        a1[k, za] = yp[k, core, 0]
        b1[k, xa] = yp[k, core, 1]

        def exchange(far, source, dst, ss, rs):
            return [send(source(d[2]), dst, ss.at[k, i], rs.at[k, i], rows_peer(*d)) for i, d in enumerate(far)]

        a_copies = exchange(z_far, lambda dc: yp.at[k, lax.rem(core + dc, 2), 0], a1.at[k, za], a1_ss, a1_rs)
        b_copies = exchange(x_far, lambda dc: yp.at[k, lax.rem(core + dc, 2), 1], b1.at[k, xa], b1_ss, b1_rs)
        for copy in b_copies:
            copy.wait_recv()
        b2[k, za] = add_all([b1[k, i] for i in range(2 * NX)]).astype(BF16)
        b_copies = exchange(z_far, lambda dc: b2.at[k, za], b2.at[k, za], b2_ss, b2_rs)
        for copy in a_copies:
            copy.wait_recv()
        a2[k, xa] = add_all([a1[k, i] for i in range(4)]).astype(BF16)
        a_copies = exchange(x_far, lambda dc: a2.at[k, xa], a2.at[k, xa], a2_ss, a2_rs)
        for copy in a_copies + b_copies:
            copy.wait_recv()
        q = jnp.concatenate([
            jnp.concatenate([
                add_all([a2[k, i * 2 + c] for i in range(NX)]).astype(BF16),
                add_all([b2[k, i * 2 + c] for i in range(2)]).astype(BF16)], axis=1)
            for c in range(2)], axis=0)

    gc[0, params] = gram(q)
    for i, t in enumerate(others):
        send(gc.at[0, params], gc.at[0, params], gc_ss.at[i], gc_rs.at[0, params], device(*t))
    for copy in pending[: -len(others)]:
        copy.wait_send()
    for t in others:
        await_from(gc, gc_rs, 0, t)
    total = gc[0, 0]
    for i in range(1, NY * NZ):
        total = total + gc[0, i]
    out[...] = apply(split_inverse(total), q).astype(BF16)
    for copy in pending[-len(others) :]:
        copy.wait_send()


def local(jacobian, pattern, row_class, class_weight, probes):
    nrows, ncols = jacobian.shape
    k, n, half = ITERS, NY * NZ, ncols // 2
    vmem, dma = pltpu.VMEM, pltpu.SemaphoreType.DMA
    return pl.pallas_call(
        kernel,
        out_shape=jax.ShapeDtypeStruct(probes.shape, BF16),
        in_specs=[pl.BlockSpec(memory_space=pl.ANY)] * 5,
        out_specs=pl.BlockSpec(memory_space=pltpu.VMEM),
        scratch_shapes=[
            pltpu.SMEM(pattern.shape[::-1], jnp.int32), pltpu.SMEM(class_weight.shape, F32),
            vmem((nrows // 128, 128), jnp.int32), vmem(probes.shape, BF16),
            vmem((nrows, ncols), BF16), vmem((NZ, 1, nrows // NZ), F32), vmem((nrows // 128, 128), F32),
            vmem((128, ncols), BF16), vmem((NY, 32, BLOCK), F32),
            vmem((k, NZ, NY, 32, BLOCK), BF16), vmem((k, n, 32, BLOCK), BF16), vmem((k, n, 32, BLOCK), BF16),
            vmem((k - 1, NY, 8, 128), F32), vmem((k - 1, NZ, 8, 128), F32), vmem((1, n, 8, 128), F32),
            vmem((k, 2, 2, 16, half), BF16), vmem((k, 4, 16, half), BF16), vmem((k, 2 * NX, 16, half), BF16),
            vmem((k, 2 * NX, 16, half), BF16), vmem((k, 4, 16, half), BF16),
            dma((NZ,)), dma((4,)),
            dma((k, n - 1)), dma((k, n)), dma((k, n - 1)), dma((k, n)),
            dma((k - 1, 3)), dma((k - 1, 3)), dma((k - 1, 3)), dma((k - 1, 3)), dma((n - 1,)), dma((1, n)),
            dma((k, 3)), dma((k, 3)), dma((k, 7)), dma((k, 7)), dma((k, 7)), dma((k, 7)), dma((k, 3)), dma((k, 3)),
        ],
        compiler_params=pltpu.CompilerParams(collective_id=0, has_side_effects=True, vmem_limit_bytes=32 * 2**20),
    )(*(pltpu.with_memory_space_constraint(a, pltpu.HBM)
        for a in (pattern.T, class_weight, jacobian, row_class.reshape(-1, 128), probes)))


def solution(mesh):
    placed = (P("rows", "params"), P("rows", "params"), P("rows"), P(), P(None, "params"))
    return jax.shard_map(
        local, mesh=mesh, in_specs=placed, out_specs=P(None, "params"), check_vma=False
    )
```

```python
import functools
import math

import jax
import jax.numpy as jnp
from jax import lax
from jax.experimental import pallas as pl
from jax.experimental.pallas import tpu as pltpu
from jax.sharding import PartitionSpec as P

P_SIZE = 12288
BLOCK = 128
ITERS = 4
NY, NZ, NX = 4, 4, 4
MESH = pl.DeviceIdType.MESH
BF16, F32 = jnp.bfloat16, jnp.float32


def dot_t(a, b):
    return lax.dot_general(a, b, (((1,), (1,)), ((), ())), preferred_element_type=F32)


def dot(a, b):
    return jnp.dot(a, b, preferred_element_type=F32)


def add_all(terms):
    total = terms[0].astype(F32)
    for term in terms[1:]:
        total = total + term.astype(F32)
    return total


def pack_gram(g):
    return g[0:8] + pltpu.roll(g[8:16], 32, 1) + pltpu.roll(g[16:24], 64, 1) + pltpu.roll(g[24:32], 96, 1)


def scaled_inverse(gp, scale):
    tile = gp.shape
    row = lax.broadcasted_iota(jnp.int32, tile, 0)
    lane = lax.broadcasted_iota(jnp.int32, tile, 1)
    nb, n = 4, 32
    b = []
    for i in range(nb):
        a = pltpu.roll(gp, 128 - 32 * i, 1) if i else gp
        b.append(jnp.where(lane < n, a, jnp.where(lane - n == row + 8 * i, 1.0, 0.0)))

    def spread(v):
        return jnp.broadcast_to(v, tile)

    for g in range(nb):
        col = {i: [spread(b[i][:, 8 * g + k : 8 * g + k + 1]) for k in range(8)] for i in range(g, nb)}
        r = [spread(b[g][m : m + 1, :]) for m in range(8)]
        a = {(m, k): spread(col[g][k][m : m + 1, :]) for m in range(8) for k in range(m + 1)}
        for k in range(8):
            inv = 1.0 / a[k, k]
            for i in range(g + 1, nb):
                factor = col[i][k] * inv
                b[i] = b[i] - factor * r[k]
                for m in range(k + 1, 8):
                    col[i][m] = col[i][m] - factor * a[m, k]
            for m in range(k + 1, 8):
                factor = a[m, k] * inv
                r[m] = r[m] - factor * r[k]
                for l in range(k + 1, m + 1):
                    a[m, l] = a[m, l] - factor * a[l, k]
        for m in range(8):
            b[g] = jnp.where(row == m, r[m], b[g])
    out = []
    for i in range(nb):
        diag = jnp.sum(jnp.where(lane == row + 8 * i, b[i], 0.0), axis=1, keepdims=True)
        out.append(pltpu.roll(b[i], 128 - n, 1) * (lax.rsqrt(diag) * scale))
    return jnp.concatenate(out, axis=0)[:, :n]


def kernel(pattern_h, class_weight_h, jac, row_class_h, probes_h, out, pattern, class_weight, row_class, probes, m, w, w16, qpad, zown,
           za_s, za_r, zc, ga, gb, gc, yp, a1, a2, b1, b2, load_sem, in_sem,
           za_ss, za_rs, zc_ss, zc_rs, ga_ss, ga_rs, gb_ss, gb_rs, gc_ss, gc_rs,
           a1_ss, a1_rs, a2_ss, a2_rs, b1_ss, b1_rs, b2_ss, b2_rs):
    rows, params = lax.axis_index("rows"), lax.axis_index("params")
    y, zl = lax.rem(params, NY), lax.div(params, NY)
    core, zh, x = lax.rem(rows, 2), lax.rem(lax.div(rows, 2), 2), lax.div(rows, 4)
    group = m.shape[1]
    per = group // BLOCK
    half = m.shape[2] // 2
    scale = math.sqrt(P_SIZE)
    pending = []

    def yz_peer(dz, dy):
        return {"params": lax.rem(zl + dz, NZ) * NY + lax.rem(y + dy, NY)}

    def rows_peer(dx, dz, dc):
        return {"rows": lax.rem(x + dx, NX) * 4 + lax.rem(zh + dz, 2) * 2 + lax.rem(core + dc, 2)}

    def device(tz, ty):
        return {"params": tz * NY + ty}

    low = 1 - lax.div(zl, 2)
    z_order = [3 * low, 1 + low, zl + 1 - 2 * lax.rem(zl, 2), zl]
    y_order = [lax.rem(y + dy, NY) for dy in (2, 1, 3, 0)]
    others = [(tz, ty) for tz in z_order for ty in y_order][:-1]
    z_far = [(0, 1, 1), (0, 1, 0), (0, 0, 1)]
    x_far = [(2, 0, 1), (2, 0, 0), (1, 0, 1), (3, 0, 1), (1, 0, 0), (3, 0, 0), (0, 0, 1)]

    def send(src, dst, ssem, rsem, peer):
        copy = pltpu.make_async_remote_copy(
            src_ref=src, dst_ref=dst, send_sem=ssem, recv_sem=rsem, device_id=peer, device_id_type=MESH)
        copy.start()
        pending.append(copy)
        return copy

    inputs = [pltpu.make_async_copy(src, dst, in_sem.at[i]) for i, (src, dst) in enumerate(
        ((pattern_h, pattern), (probes_h, probes), (row_class_h, row_class), (class_weight_h, class_weight)))]
    loads = []
    for i, c in enumerate(z_order):
        at = pl.ds(pl.multiple_of(c * group, group), group)
        loads.append(pltpu.make_async_copy(jac.at[at, :], m.at[i], load_sem.at[i]))
    inputs[0].start()
    inputs[1].start()
    loads[0].start()
    inputs[2].start()
    inputs[3].start()
    for copy in loads[1:]:
        copy.start()

    barrier = pltpu.get_barrier_semaphore()
    friends = [device(*t) for t in others] + [rows_peer(*d) for d in z_far + x_far[:-1]]
    for peer in friends:
        pl.semaphore_signal(barrier, inc=1, device_id=peer, device_id_type=MESH)

    def prepare(i):
        c = z_order[i]
        for r in range(per):
            for j in range(pattern.shape[0]):
                keep = jnp.full((BLOCK, BLOCK), pattern[j, c * per + r].astype(F32)).astype(BF16)
                at = (i, pl.ds(r * BLOCK, BLOCK), pl.ds(j * BLOCK, BLOCK))
                m[at] = m[at] * keep

    def weigh():
        inputs[2].wait()
        inputs[3].wait()
        classes = row_class[...]
        weight = jnp.zeros(classes.shape, F32)
        for c in range(class_weight.shape[0]):
            weight = jnp.where(classes == c, class_weight[c], weight)
        w16[...] = weight
        for c in range(NZ):
            for i in range(per):
                w[c, :, i * BLOCK : (i + 1) * BLOCK] = w16[c * per + i : c * per + i + 1, :]

    def raw_z(k, q, n):
        part = dot_t(q, m[n])
        for i in range(NY):
            block = part[:, i * BLOCK : (i + 1) * BLOCK]
            za_s[k, n, i] = block.astype(BF16)
            if n == NZ - 1:
                zown[i] = block

    def scatter_z(k, n):
        for i in range(n * NY, min((n + 1) * NY, len(others))):
            tz, ty = others[i]
            send(za_s.at[k, n, ty], za_r.at[k, params], za_ss.at[k, i], za_rs.at[k, params], device(tz, ty))

    def await_from(buf, sem, k, t):
        p = t[0] * NY + t[1]
        pltpu.make_async_remote_copy(
            src_ref=buf.at[k, p], dst_ref=buf.at[k, p], send_sem=sem.at[k, p], recv_sem=sem.at[k, p],
            device_id=device(*t), device_id_type=MESH).wait_recv()
        return p

    def gram(q):
        qpad[0:32, :] = q
        return pack_gram(dot_t(q, qpad[...]))

    def scatter_gram(k, q):
        ga[k, y] = gram(q)
        return [send(ga.at[k, y], ga.at[k, y], ga_ss.at[k, d - 1], ga_rs.at[k, d - 1], yz_peer(0, d))
                for d in (2, 1, 3)]

    def forward_gram(k, copies):
        for copy in copies:
            copy.wait_recv()
        gb[k, zl] = ((ga[k, 0] + ga[k, 1]) + ga[k, 2]) + ga[k, 3]
        return [send(gb.at[k, zl], gb.at[k, zl], gb_ss.at[k, d - 1], gb_rs.at[k, d - 1], yz_peer(d, 0))
                for d in (2, 3, 1)]

    def split_inverse(g):
        inv = scaled_inverse(g, scale)
        high = inv.astype(BF16)
        low = (inv - high.astype(F32)).astype(BF16)
        return jnp.concatenate([high, low], axis=0)

    def apply(inv2, v):
        u = dot(inv2, v)
        return u[:32] + u[32:]

    inputs[1].wait()
    inputs[0].wait()
    q = probes[...]
    for k in range(ITERS):
        if k == 0:
            loads[0].wait()
            prepare(0)
        for n in range(NZ):
            if k == 0 and n < NZ - 1:
                loads[n + 1].wait()
            raw_z(k, q, n)
            if k == 0 and n < NZ - 1:
                prepare(n + 1)
            if k == 0 and n == NZ - 1:
                pl.semaphore_wait(barrier, len(friends))
                for i in range(NZ):
                    scatter_z(k, i)
            if k > 0:
                scatter_z(k, n)
            if k > 0 and n == 1:
                g_copies = scatter_gram(k - 1, q)
        if k == 0:
            weigh()
            qpad[...] = jnp.zeros_like(qpad)
        else:
            g_copies = forward_gram(k - 1, g_copies)
        total = zown[y]
        for t in reversed(others):
            total = total + za_r[k, await_from(za_r, za_rs, k, t)].astype(F32)
        zc[k, params] = total.astype(BF16)
        for i, t in enumerate(others):
            send(zc.at[k, params], zc.at[k, params], zc_ss.at[k, i], zc_rs.at[k, params], device(*t))
        if k > 0:
            for copy in g_copies:
                copy.wait_recv()
            inv2 = split_inverse(((gb[k - 1, 0] + gb[k - 1, 1]) + gb[k - 1, 2]) + gb[k - 1, 3])
        acc = None
        for n in reversed(range(NZ)):
            c = z_order[n]
            for t in others[n * NY : (n + 1) * NY]:
                await_from(zc, zc_rs, k, t)
            z = jnp.concatenate([zc[k, c * NY + i] for i in range(NY)], axis=1)
            z = z.astype(F32) if k == 0 else apply(inv2, z)
            v = (z * w[c]).astype(BF16)
            part = dot(v, m[n])
            acc = part if acc is None else acc + part
        for h in range(2):
            for f in range(2):
                yp[k, h, f] = acc[16 * h : 16 * h + 16, half * f : half * f + half].astype(BF16)
        za, xa = zh * 2 + core, x * 2 + core
        a1[k, za] = yp[k, core, 0]
        b1[k, xa] = yp[k, core, 1]

        def exchange(far, source, dst, ss, rs):
            return [send(source(d[2]), dst, ss.at[k, i], rs.at[k, i], rows_peer(*d)) for i, d in enumerate(far)]

        a_copies = exchange(z_far, lambda dc: yp.at[k, lax.rem(core + dc, 2), 0], a1.at[k, za], a1_ss, a1_rs)
        b_copies = exchange(x_far, lambda dc: yp.at[k, lax.rem(core + dc, 2), 1], b1.at[k, xa], b1_ss, b1_rs)
        for copy in b_copies:
            copy.wait_recv()
        b2[k, za] = add_all([b1[k, i] for i in range(2 * NX)]).astype(BF16)
        b_copies = exchange(z_far, lambda dc: b2.at[k, za], b2.at[k, za], b2_ss, b2_rs)
        for copy in a_copies:
            copy.wait_recv()
        a2[k, xa] = add_all([a1[k, i] for i in range(4)]).astype(BF16)
        a_copies = exchange(x_far, lambda dc: a2.at[k, xa], a2.at[k, xa], a2_ss, a2_rs)
        for copy in a_copies + b_copies:
            copy.wait_recv()
        q = jnp.concatenate([
            jnp.concatenate([
                add_all([a2[k, i * 2 + c] for i in range(NX)]).astype(BF16),
                add_all([b2[k, i * 2 + c] for i in range(2)]).astype(BF16)], axis=1)
            for c in range(2)], axis=0)

    gc[0, params] = gram(q)
    for i, t in enumerate(others):
        send(gc.at[0, params], gc.at[0, params], gc_ss.at[i], gc_rs.at[0, params], device(*t))
    for copy in pending[: -len(others)]:
        copy.wait_send()
    for t in others:
        await_from(gc, gc_rs, 0, t)
    total = gc[0, 0]
    for i in range(1, NY * NZ):
        total = total + gc[0, i]
    out[...] = apply(split_inverse(total), q).astype(BF16)
    for copy in pending[-len(others) :]:
        copy.wait_send()


def local(jacobian, pattern, row_class, class_weight, probes):
    nrows, ncols = jacobian.shape
    k, n, half = ITERS, NY * NZ, ncols // 2
    vmem, dma = pltpu.VMEM, pltpu.SemaphoreType.DMA
    return pl.pallas_call(
        kernel,
        out_shape=jax.ShapeDtypeStruct(probes.shape, BF16),
        in_specs=[pl.BlockSpec(memory_space=pl.ANY)] * 5,
        out_specs=pl.BlockSpec(memory_space=pltpu.VMEM),
        scratch_shapes=[
            pltpu.SMEM(pattern.shape[::-1], jnp.int32), pltpu.SMEM(class_weight.shape, F32),
            vmem((nrows // 128, 128), jnp.int32), vmem(probes.shape, BF16),
            vmem((NZ, nrows // NZ, ncols), BF16), vmem((NZ, 1, nrows // NZ), F32), vmem((nrows // 128, 128), F32),
            vmem((128, ncols), BF16), vmem((NY, 32, BLOCK), F32),
            vmem((k, NZ, NY, 32, BLOCK), BF16), vmem((k, n, 32, BLOCK), BF16), vmem((k, n, 32, BLOCK), BF16),
            vmem((k - 1, NY, 8, 128), F32), vmem((k - 1, NZ, 8, 128), F32), vmem((1, n, 8, 128), F32),
            vmem((k, 2, 2, 16, half), BF16), vmem((k, 4, 16, half), BF16), vmem((k, 2 * NX, 16, half), BF16),
            vmem((k, 2 * NX, 16, half), BF16), vmem((k, 4, 16, half), BF16),
            dma((NZ,)), dma((4,)),
            dma((k, n - 1)), dma((k, n)), dma((k, n - 1)), dma((k, n)),
            dma((k - 1, 3)), dma((k - 1, 3)), dma((k - 1, 3)), dma((k - 1, 3)), dma((n - 1,)), dma((1, n)),
            dma((k, 3)), dma((k, 3)), dma((k, 7)), dma((k, 7)), dma((k, 7)), dma((k, 7)), dma((k, 3)), dma((k, 3)),
        ],
        compiler_params=pltpu.CompilerParams(collective_id=0, has_side_effects=True, vmem_limit_bytes=32 * 2**20),
    )(*(pltpu.with_memory_space_constraint(a, pltpu.HBM)
        for a in (pattern.T, class_weight, jacobian, row_class.reshape(-1, 128), probes)))


def solution(mesh):
    placed = (P("rows", "params"), P("rows", "params"), P("rows"), P(), P(None, "params"))
    return jax.shard_map(
        local, mesh=mesh, in_specs=placed, out_specs=P(None, "params"), check_vma=False
    )
```

```python
import functools
import math

import jax
import jax.numpy as jnp
from jax import lax
from jax.experimental import pallas as pl
from jax.experimental.pallas import tpu as pltpu
from jax.sharding import PartitionSpec as P

P_SIZE = 12288
BLOCK = 128
ITERS = 4
NY, NZ, NX = 4, 4, 4
MESH = pl.DeviceIdType.MESH
BF16, F32 = jnp.bfloat16, jnp.float32


def dot_t(a, b):
    return lax.dot_general(a, b, (((1,), (1,)), ((), ())), preferred_element_type=F32)


def dot(a, b):
    return jnp.dot(a, b, preferred_element_type=F32)


def add_all(terms):
    total = terms[0].astype(F32)
    for term in terms[1:]:
        total = total + term.astype(F32)
    return total


def pack_gram(g):
    return g[0:8] + pltpu.roll(g[8:16], 32, 1) + pltpu.roll(g[16:24], 64, 1) + pltpu.roll(g[24:32], 96, 1)


def scaled_inverse(gp, scale):
    tile = gp.shape
    row = lax.broadcasted_iota(jnp.int32, tile, 0)
    lane = lax.broadcasted_iota(jnp.int32, tile, 1)
    nb, n = 4, 32
    b = []
    for i in range(nb):
        a = pltpu.roll(gp, 128 - 32 * i, 1) if i else gp
        b.append(jnp.where(lane < n, a, jnp.where(lane - n == row + 8 * i, 1.0, 0.0)))

    def spread(v):
        return jnp.broadcast_to(v, tile)

    for g in range(nb):
        col = {i: [spread(b[i][:, 8 * g + k : 8 * g + k + 1]) for k in range(8)] for i in range(g, nb)}
        r = [spread(b[g][m : m + 1, :]) for m in range(8)]
        a = {(m, k): spread(col[g][k][m : m + 1, :]) for m in range(8) for k in range(m + 1)}
        for k in range(8):
            inv = 1.0 / a[k, k]
            for i in range(g + 1, nb):
                factor = col[i][k] * inv
                b[i] = b[i] - factor * r[k]
                for m in range(k + 1, 8):
                    col[i][m] = col[i][m] - factor * a[m, k]
            for m in range(k + 1, 8):
                factor = a[m, k] * inv
                r[m] = r[m] - factor * r[k]
                for l in range(k + 1, m + 1):
                    a[m, l] = a[m, l] - factor * a[l, k]
        for m in range(8):
            b[g] = jnp.where(row == m, r[m], b[g])
    out = []
    for i in range(nb):
        diag = jnp.sum(jnp.where(lane == row + 8 * i, b[i], 0.0), axis=1, keepdims=True)
        out.append(pltpu.roll(b[i], 128 - n, 1) * (lax.rsqrt(diag) * scale))
    return jnp.concatenate(out, axis=0)[:, :n]


def kernel(pattern_h, class_weight_h, jac, row_class_h, probes_h, out, pattern, class_weight, row_class, probes, m, w, w16, qpad, zown,
           za_s, za_r, zc, ga, gb, gc, yp, a1, a2, b1, b2, load_sem, in_sem,
           za_ss, za_rs, zc_ss, zc_rs, ga_ss, ga_rs, gb_ss, gb_rs, gc_ss, gc_rs,
           a1_ss, a1_rs, a2_ss, a2_rs, b1_ss, b1_rs, b2_ss, b2_rs):
    rows, params = lax.axis_index("rows"), lax.axis_index("params")
    y, zl = lax.rem(params, NY), lax.div(params, NY)
    core, zh, x = lax.rem(rows, 2), lax.rem(lax.div(rows, 2), 2), lax.div(rows, 4)
    group = m.shape[1]
    per = group // BLOCK
    half = m.shape[2] // 2
    scale = math.sqrt(P_SIZE)
    pending = []

    def yz_peer(dz, dy):
        return {"params": lax.rem(zl + dz, NZ) * NY + lax.rem(y + dy, NY)}

    def rows_peer(dx, dz, dc):
        return {"rows": lax.rem(x + dx, NX) * 4 + lax.rem(zh + dz, 2) * 2 + lax.rem(core + dc, 2)}

    def device(tz, ty):
        return {"params": tz * NY + ty}

    low = 1 - lax.div(zl, 2)
    z_order = [3 * low, 1 + low, zl + 1 - 2 * lax.rem(zl, 2), zl]
    y_order = [lax.rem(y + dy, NY) for dy in (2, 1, 3, 0)]
    others = [(tz, ty) for tz in z_order for ty in y_order][:-1]
    z_far = [(0, 1, 1), (0, 1, 0), (0, 0, 1)]
    x_far = [(2, 0, 1), (2, 0, 0), (1, 0, 1), (3, 0, 1), (1, 0, 0), (3, 0, 0), (0, 0, 1)]

    def send(src, dst, ssem, rsem, peer):
        copy = pltpu.make_async_remote_copy(
            src_ref=src, dst_ref=dst, send_sem=ssem, recv_sem=rsem, device_id=peer, device_id_type=MESH)
        copy.start()
        pending.append(copy)
        return copy

    inputs = [pltpu.make_async_copy(src, dst, in_sem.at[i]) for i, (src, dst) in enumerate(
        ((pattern_h, pattern), (probes_h, probes), (row_class_h, row_class), (class_weight_h, class_weight)))]
    loads = []
    for i, c in enumerate(z_order):
        at = pl.ds(pl.multiple_of(c * group, group), group)
        loads.append(pltpu.make_async_copy(jac.at[at, :], m.at[i], load_sem.at[i]))
    inputs[0].start()
    inputs[1].start()
    loads[0].start()
    inputs[2].start()
    inputs[3].start()
    for copy in loads[1:]:
        copy.start()

    barrier = pltpu.get_barrier_semaphore()
    friends = [device(*t) for t in others] + [rows_peer(*d) for d in z_far + x_far[:-1]]
    for peer in friends:
        pl.semaphore_signal(barrier, inc=1, device_id=peer, device_id_type=MESH)

    def prepare(i):
        c = z_order[i]
        for r in range(per):
            for j in range(pattern.shape[0]):
                keep = jnp.full((BLOCK, BLOCK), pattern[j, c * per + r].astype(F32)).astype(BF16)
                at = (i, pl.ds(r * BLOCK, BLOCK), pl.ds(j * BLOCK, BLOCK))
                m[at] = m[at] * keep

    def weigh():
        inputs[2].wait()
        inputs[3].wait()
        classes = row_class[...]
        weight = jnp.zeros(classes.shape, F32)
        for c in range(class_weight.shape[0]):
            weight = jnp.where(classes == c, class_weight[c], weight)
        w16[...] = weight
        for c in range(NZ):
            for i in range(per):
                w[c, :, i * BLOCK : (i + 1) * BLOCK] = w16[c * per + i : c * per + i + 1, :]

    def raw_z(k, q, n):
        part = dot_t(q, m[n])
        for i in range(NY):
            block = part[:, i * BLOCK : (i + 1) * BLOCK]
            za_s[k, n, i] = block.astype(BF16)
            if n == NZ - 1:
                zown[i] = block

    def scatter_z(k, n):
        for i in range(n * NY, min((n + 1) * NY, len(others))):
            tz, ty = others[i]
            send(za_s.at[k, n, ty], za_r.at[k, params], za_ss.at[k, i], za_rs.at[k, params], device(tz, ty))

    def await_from(buf, sem, k, t):
        p = t[0] * NY + t[1]
        pltpu.make_async_remote_copy(
            src_ref=buf.at[k, p], dst_ref=buf.at[k, p], send_sem=sem.at[k, p], recv_sem=sem.at[k, p],
            device_id=device(*t), device_id_type=MESH).wait_recv()
        return p

    def gram(q):
        qpad[0:32, :] = q
        return pack_gram(dot_t(q, qpad[...]))

    def scatter_gram(k, q):
        ga[k, y] = gram(q)
        return [send(ga.at[k, y], ga.at[k, y], ga_ss.at[k, d - 1], ga_rs.at[k, d - 1], yz_peer(0, d))
                for d in (2, 1, 3)]

    def forward_gram(k, copies):
        for copy in copies:
            copy.wait_recv()
        gb[k, zl] = ((ga[k, 0] + ga[k, 1]) + ga[k, 2]) + ga[k, 3]
        return [send(gb.at[k, zl], gb.at[k, zl], gb_ss.at[k, d - 1], gb_rs.at[k, d - 1], yz_peer(d, 0))
                for d in (2, 3, 1)]

    def split_inverse(g):
        inv = scaled_inverse(g, scale)
        high = inv.astype(BF16)
        low = (inv - high.astype(F32)).astype(BF16)
        return jnp.concatenate([high, low], axis=0)

    def apply(inv2, v):
        u = dot(inv2, v)
        return u[:32] + u[32:]

    inputs[1].wait()
    inputs[0].wait()
    q = probes[...]
    for k in range(ITERS):
        if k == 0:
            loads[0].wait()
            prepare(0)
        for n in range(NZ):
            if k == 0 and n < NZ - 1:
                loads[n + 1].wait()
            raw_z(k, q, n)
            if k == 0 and n < NZ - 1:
                prepare(n + 1)
            if k == 0 and n == NZ - 1:
                pl.semaphore_wait(barrier, len(friends))
                for i in range(NZ):
                    scatter_z(k, i)
            if k > 0:
                scatter_z(k, n)
            if k > 0 and n == NZ - 1:
                g_copies = scatter_gram(k - 1, q)
        if k == 0:
            weigh()
            qpad[...] = jnp.zeros_like(qpad)
        else:
            g_copies = forward_gram(k - 1, g_copies)
        total = zown[y]
        for t in reversed(others):
            total = total + za_r[k, await_from(za_r, za_rs, k, t)].astype(F32)
        zc[k, params] = total.astype(BF16)
        for i in (0, 1, 2, 4, 5, 6, 8, 3, 9, 10, 7, 12, 11, 13, 14):
            t = others[i]
            send(zc.at[k, params], zc.at[k, params], zc_ss.at[k, i], zc_rs.at[k, params], device(*t))
        if k > 0:
            for copy in g_copies:
                copy.wait_recv()
            inv2 = split_inverse(((gb[k - 1, 0] + gb[k - 1, 1]) + gb[k - 1, 2]) + gb[k - 1, 3])
        acc = None
        for n in reversed(range(NZ)):
            c = z_order[n]
            for t in others[n * NY : (n + 1) * NY]:
                await_from(zc, zc_rs, k, t)
            z = jnp.concatenate([zc[k, c * NY + i] for i in range(NY)], axis=1)
            z = z.astype(F32) if k == 0 else apply(inv2, z)
            v = (z * w[c]).astype(BF16)
            part = dot(v, m[n])
            acc = part if acc is None else acc + part
        for h in range(2):
            for f in range(2):
                yp[k, h, f] = acc[16 * h : 16 * h + 16, half * f : half * f + half].astype(BF16)
        za, xa = zh * 2 + core, x * 2 + core
        a1[k, za] = yp[k, core, 0]
        b1[k, xa] = yp[k, core, 1]

        def exchange(far, source, dst, ss, rs):
            return [send(source(d[2]), dst, ss.at[k, i], rs.at[k, i], rows_peer(*d)) for i, d in enumerate(far)]

        a_copies = exchange(z_far, lambda dc: yp.at[k, lax.rem(core + dc, 2), 0], a1.at[k, za], a1_ss, a1_rs)
        b_copies = exchange(x_far, lambda dc: yp.at[k, lax.rem(core + dc, 2), 1], b1.at[k, xa], b1_ss, b1_rs)
        for copy in b_copies:
            copy.wait_recv()
        b2[k, za] = add_all([b1[k, i] for i in range(2 * NX)]).astype(BF16)
        b_copies = exchange(z_far, lambda dc: b2.at[k, za], b2.at[k, za], b2_ss, b2_rs)
        for copy in a_copies:
            copy.wait_recv()
        a2[k, xa] = add_all([a1[k, i] for i in range(4)]).astype(BF16)
        a_copies = exchange(x_far, lambda dc: a2.at[k, xa], a2.at[k, xa], a2_ss, a2_rs)
        for copy in a_copies + b_copies:
            copy.wait_recv()
        q = jnp.concatenate([
            jnp.concatenate([
                add_all([a2[k, i * 2 + c] for i in range(NX)]).astype(BF16),
                add_all([b2[k, i * 2 + c] for i in range(2)]).astype(BF16)], axis=1)
            for c in range(2)], axis=0)

    gc[0, params] = gram(q)
    for i, t in enumerate(others):
        send(gc.at[0, params], gc.at[0, params], gc_ss.at[i], gc_rs.at[0, params], device(*t))
    for copy in pending[: -len(others)]:
        copy.wait_send()
    for t in others:
        await_from(gc, gc_rs, 0, t)
    total = gc[0, 0]
    for i in range(1, NY * NZ):
        total = total + gc[0, i]
    out[...] = apply(split_inverse(total), q).astype(BF16)
    for copy in pending[-len(others) :]:
        copy.wait_send()


def local(jacobian, pattern, row_class, class_weight, probes):
    nrows, ncols = jacobian.shape
    k, n, half = ITERS, NY * NZ, ncols // 2
    vmem, dma = pltpu.VMEM, pltpu.SemaphoreType.DMA
    return pl.pallas_call(
        kernel,
        out_shape=jax.ShapeDtypeStruct(probes.shape, BF16),
        in_specs=[pl.BlockSpec(memory_space=pl.ANY)] * 5,
        out_specs=pl.BlockSpec(memory_space=pltpu.VMEM),
        scratch_shapes=[
            pltpu.SMEM(pattern.shape[::-1], jnp.int32), pltpu.SMEM(class_weight.shape, F32),
            vmem((nrows // 128, 128), jnp.int32), vmem(probes.shape, BF16),
            vmem((NZ, nrows // NZ, ncols), BF16), vmem((NZ, 1, nrows // NZ), F32), vmem((nrows // 128, 128), F32),
            vmem((128, ncols), BF16), vmem((NY, 32, BLOCK), F32),
            vmem((k, NZ, NY, 32, BLOCK), BF16), vmem((k, n, 32, BLOCK), BF16), vmem((k, n, 32, BLOCK), BF16),
            vmem((k - 1, NY, 8, 128), F32), vmem((k - 1, NZ, 8, 128), F32), vmem((1, n, 8, 128), F32),
            vmem((k, 2, 2, 16, half), BF16), vmem((k, 4, 16, half), BF16), vmem((k, 2 * NX, 16, half), BF16),
            vmem((k, 2 * NX, 16, half), BF16), vmem((k, 4, 16, half), BF16),
            dma((NZ,)), dma((4,)),
            dma((k, n - 1)), dma((k, n)), dma((k, n - 1)), dma((k, n)),
            dma((k - 1, 3)), dma((k - 1, 3)), dma((k - 1, 3)), dma((k - 1, 3)), dma((n - 1,)), dma((1, n)),
            dma((k, 3)), dma((k, 3)), dma((k, 7)), dma((k, 7)), dma((k, 7)), dma((k, 7)), dma((k, 3)), dma((k, 3)),
        ],
        compiler_params=pltpu.CompilerParams(collective_id=0, has_side_effects=True, vmem_limit_bytes=32 * 2**20),
    )(*(pltpu.with_memory_space_constraint(a, pltpu.HBM)
        for a in (pattern.T, class_weight, jacobian, row_class.reshape(-1, 128), probes)))


def solution(mesh):
    placed = (P("rows", "params"), P("rows", "params"), P("rows"), P(), P(None, "params"))
    return jax.shard_map(
        local, mesh=mesh, in_specs=placed, out_specs=P(None, "params"), check_vma=False
    )
```
